256 devices in a mesh: row: 8 (over y_lo, x), col: 32 (over z, y_hi, core).
Axes of the slice: x: 4, y: 4 (y_hi: 2, y_lo: 2; y = y_hi * 2 + y_lo), z: 8, core: 2. Of those that a mesh axis runs over, the one named last changes fastest.
Arguments:
- pair_rep: float32 [256, 256, 128], P('row', 'col'), may hold values from -160 to 160
- ln_gain: float32 [128], replicated, may hold values from 0.25 to 1.75
- ln_bias: float32 [128], replicated, may hold values from -3 to 3
- w_in: float32 [1024, 128], replicated, may hold values from -0.5 to 0.5
- w_out: float32 [512, 128], replicated, may hold values from -0.25 to 0.25
- w_pde: float32 [128, 64], replicated, may hold values from -2 to 2
- labels: int32 [256, 256], P('row', 'col'), may hold values from 0 to 63
- pair_mask: int32 [256, 256], P('row', 'col'), may hold values from 0 to 1, as said below
Outputs:
- mean_loss: float32 [], replicated
- d_pair_rep: float32 [256, 256, 128], P('row', 'col')
- d_ln_gain: float32 [128], replicated
- d_ln_bias: float32 [128], replicated
- d_w_in: float32 [1024, 128], P(('row', 'col'))
- d_w_out: float32 [512, 128], P(('row', 'col'))
- d_w_pde: float32 [128, 64], replicated
The draws below stay inside these ranges and needn't reach their ends.
Inputs may be any that keep to these rules, and one draw needn't show every extreme that they name: pair_mask[i][j] = m_i m_j for a flag m_i of token i, with m_i = 1 whenever i is a multiple of 16.
All inputs are finite; a program needn't handle non-finite values.
Results may differ from the reference program's by a relative error of at most 0.0003.
Values sent between devices are 32-bit elements; how exact they have to be, the bound alone decides.
No kernel may reach another device: no remote copies, remote signals or barrier semaphores. Data moves between devices by JAX's collectives and lax.ppermute only.
A program may use at most 64 MiB of HBM per device.

```python
import jax
import jax.numpy as jnp
from jax import lax

C = 128
H = 512
BINS = 64
TOKENS = 256


def draw_pair_rep(key, part):
    keys = jax.random.split(jax.random.fold_in(key, 11), 1)
    values = jax.random.normal(keys[0], (TOKENS, TOKENS, C), jnp.float32)
    return jnp.clip(values, -6.0, 6.0)


def draw_w_pde(key, part):
    keys = jax.random.split(jax.random.fold_in(key, 23), 1)
    values = jax.random.normal(keys[0], (C, BINS), jnp.float32) * (2.5 / C ** 0.5)
    return jnp.clip(values, -2.0, 2.0)


def draw_pair_mask(key, part):
    position = jnp.arange(TOKENS, dtype=jnp.int32)
    threshold = 300 + 650 * position // TOKENS
    ticket = jax.random.randint(jax.random.fold_in(key, 37), (TOKENS,), 0, 1000, dtype=jnp.int32)
    resolved = jnp.logical_or(ticket < threshold, position % 16 == 0).astype(jnp.int32)
    return resolved[:, None] * resolved[None, :]


def with_ends(values, rng, smallest, high):
    place = [jax.random.randint(jax.random.fold_in(rng, axis), (), 0, length) for axis, length in enumerate(values.shape)]
    widest = values.shape.index(max(values.shape))
    beside = place[:widest] + [(place[widest] + 1) % values.shape[widest]] + place[widest + 1:]
    return values.at[tuple(place)].set(smallest).at[tuple(beside)].set(high)


def noise(rng, shape, deviation, limit, kind=jnp.bfloat16):
    array = deviation * jax.random.normal(rng, shape, jnp.float32)
    return jnp.clip(array, min=-limit, max=limit).astype(kind)


def setup_inputs(seed: int = 0) -> dict:
    seeds = jax.random.split(jax.random.key(seed), 9)
    pair_rep = draw_pair_rep(jax.random.fold_in(seeds[8], 71), 0)
    ln_gain = jnp.clip(1.0 + 0.15 * jax.random.normal(seeds[1], (C,), jnp.float32), 0.25, 1.75)
    ln_bias = noise(seeds[2], (C,), 0.5, 3.0, jnp.float32)
    w_in = noise(seeds[3], (2 * H, C), C ** -0.5, 0.5, jnp.float32)
    w_out = noise(seeds[4], (H, C), H ** -0.5, 0.25, jnp.float32)
    w_pde = draw_w_pde(jax.random.fold_in(seeds[8], 71), 0)
    labels = with_ends(jax.random.randint(seeds[6], (TOKENS, TOKENS), 0, BINS), jax.random.fold_in(seeds[6], 1), 0, BINS - 1).astype(jnp.int32)
    pair_mask = draw_pair_mask(jax.random.fold_in(seeds[8], 71), 0)
    return dict(pair_rep=pair_rep, ln_gain=ln_gain, ln_bias=ln_bias, w_in=w_in, w_out=w_out, w_pde=w_pde, labels=labels, pair_mask=pair_mask)


epsilon = 1e-05

def transition(rows_block, ln_gain, ln_bias, w_in, w_out):
    average = lax.optimization_barrier(jnp.mean(rows_block, axis=-1, keepdims=True))
    centred = rows_block - average
    variance = lax.optimization_barrier(jnp.mean(centred * centred, axis=-1, keepdims=True))
    normed = centred * lax.rsqrt(variance + epsilon) * ln_gain + ln_bias
    projected_in = lax.dot_general(normed, w_in, (((1,), (1,)), ((), ())), precision=lax.Precision.HIGHEST, preferred_element_type=jnp.float32)
    hidden_units = w_out.shape[0]
    hidden = jax.nn.silu(projected_in[:, :hidden_units]) * projected_in[:, hidden_units:]
    return rows_block + jnp.dot(hidden, w_out, precision=lax.Precision.HIGHEST, preferred_element_type=jnp.float32)

def group_rows(tile_rows, tile_cols):
    stride_rows = 1
    while stride_rows < tile_rows and stride_rows * tile_cols < 1024 and (tile_rows % (stride_rows * 2) == 0):
        stride_rows = stride_rows * 2
    return stride_rows

def reference(pair_rep, ln_gain, ln_bias, w_in, w_out, w_pde, labels, pair_mask):
    tokens_first, tokens_second, channels = pair_rep.shape
    stride_rows = group_rows(tokens_first, tokens_second)
    blocks = pair_rep.reshape(tokens_first // stride_rows, stride_rows * tokens_second, channels)

    def forward(rows_block):
        return transition(rows_block, ln_gain, ln_bias, w_in, w_out)
    updated = lax.map(forward, blocks).reshape(tokens_first, tokens_second, channels)
    projected = jnp.einsum('ijc,cb->ijb', updated, w_pde, precision=lax.Precision.HIGHEST)
    scores = projected + jnp.transpose(projected, (1, 0, 2))
    mask_float = pair_mask.astype(jnp.float32)
    valid_count = jnp.sum(mask_float)
    highest = lax.optimization_barrier(jnp.max(scores, axis=-1, keepdims=True))
    shifted = jnp.exp(scores - highest)
    exp_total = lax.optimization_barrier(jnp.sum(shifted, axis=-1, keepdims=True))
    log_total = highest + jnp.log(exp_total)
    picked = jnp.take_along_axis(scores, labels[:, :, None].astype(jnp.int32), axis=-1)
    mean_loss = jnp.sum(mask_float * (log_total - picked)[:, :, 0]) / valid_count
    bin_index = jnp.arange(scores.shape[2], dtype=jnp.int32)
    onehot = (labels[:, :, None] == bin_index[None, None, :]).astype(jnp.float32)
    d_scores = mask_float[:, :, None] * (shifted / exp_total - onehot) / valid_count
    d_sym = d_scores + jnp.transpose(d_scores, (1, 0, 2))
    d_w_pde = jnp.einsum('ijc,ijb->cb', updated, d_sym, precision=lax.Precision.HIGHEST)
    d_updated = jnp.einsum('ijb,cb->ijc', d_sym, w_pde, precision=lax.Precision.HIGHEST)
    cot_blocks = d_updated.reshape(blocks.shape)

    def backward(totals, pieces):
        rows_block, cotangent = pieces
        outcome, pullback = jax.vjp(transition, rows_block, ln_gain, ln_bias, w_in, w_out)
        gradients = pullback(cotangent)
        merged = tuple((earlier + later for earlier, later in zip(totals, gradients[1:])))
        return (merged, gradients[0])
    start_sums = (jnp.zeros_like(ln_gain), jnp.zeros_like(ln_bias), jnp.zeros_like(w_in), jnp.zeros_like(w_out))
    param_sums, d_blocks = lax.scan(backward, start_sums, (blocks, cot_blocks))
    d_pair_rep = d_blocks.reshape(pair_rep.shape)
    d_ln_gain = param_sums[0]
    d_ln_bias = param_sums[1]
    d_w_in = param_sums[2]
    d_w_out = param_sums[3]
    return (mean_loss, d_pair_rep, d_ln_gain, d_ln_bias, d_w_in, d_w_out, d_w_pde)
```

```python
import functools

import jax
import jax.numpy as jnp
from jax import lax
from jax.experimental import pallas as pl
from jax.experimental.pallas import tpu as pltpu
from jax.sharding import Mesh
from jax.sharding import PartitionSpec as P

AXES = ("yl", "x", "z", "yh", "co")
ROW = ("yl", "x")
COL = ("z", "yh", "co")
PLANE = ("yl", "x", "yh")

EPSILON = 1e-05
ROWS, COLS, C, H, BINS = 32, 8, 128, 512, 64
PAIRS = ROWS * COLS
BIG = 48
SMALL = 40
LABEL, MASK = 64, 65


def split(value):
    high = value.astype(jnp.bfloat16)
    return high, (value - high.astype(jnp.float32)).astype(jnp.bfloat16)


def dot(left, right, left_dim, right_dim):
    dims = (((left_dim,), (right_dim,)), ((), ()))
    one = functools.partial(lax.dot_general, dimension_numbers=dims, preferred_element_type=jnp.float32)
    return one(left[0], right[0]) + (one(left[0], right[1]) + one(left[1], right[0]))


def norm(x, gain, bias):
    centred = x - jnp.mean(x, axis=-1, keepdims=True)
    scale = lax.rsqrt(jnp.mean(centred * centred, axis=-1, keepdims=True) + EPSILON)
    unit = centred * scale
    return scale, unit, unit * gain + bias


def padded(w_pde):
    return jnp.concatenate([w_pde, jnp.zeros((C, C - BINS), jnp.float32)], axis=1)


def forward_kernel(base, x_ref, gain, bias, w_in, w_out, w_pde, labels, mask, send, own, hidden_ref, silu_ref, slope_ref, updated_ref):
    x = x_ref[...]
    _, _, normed = norm(x, gain[...], bias[...])
    projected_in = dot(split(normed), split(w_in[...]), 1, 1)
    gate, up = projected_in[:, :H], projected_in[:, H:]
    sigmoid = 1.0 / (1.0 + jnp.exp(-gate))
    silu = gate * sigmoid
    hidden = silu * up
    silu_ref[...] = silu
    slope_ref[...] = up * (sigmoid * (1.0 + gate * (1.0 - sigmoid)))
    hidden_ref[...] = hidden
    updated = x + dot(split(hidden), split(w_out[...]), 1, 0)
    updated_ref[...] = updated
    projected = dot(split(updated), split(padded(w_pde[...])), 1, 0)
    code = (labels[...] + 64 * mask[...]).astype(jnp.float32).astype(jnp.bfloat16)
    pair = lax.broadcasted_iota(jnp.int32, (PAIRS, ROWS), 0)
    row = lax.broadcasted_iota(jnp.int32, (PAIRS, ROWS), 1)
    spread = jnp.where(pair // COLS == row, 1.0, 0.0).astype(jnp.bfloat16)
    by_row = jnp.dot(spread, code, preferred_element_type=jnp.float32)
    pair = lax.broadcasted_iota(jnp.int32, (PAIRS, COLS), 0)
    col = lax.broadcasted_iota(jnp.int32, (PAIRS, COLS), 1)
    code = jnp.sum(jnp.where(pair % COLS == col, by_row, 0.0), axis=1, keepdims=True)
    scored = jnp.where(code >= 64.0, 1.0, 0.0)
    lane = lax.broadcasted_iota(jnp.int32, (PAIRS, C), 1)
    projected = jnp.where(lane == LABEL, code - 64.0 * scored, projected)
    projected = jnp.where(lane == MASK, scored, projected)
    own[...] = projected
    send[pl.ds(base[0], 4)] = projected.reshape(4, 64, C)
    send[pl.ds(4 - base[0], 4)] = jnp.zeros((4, 64, C), jnp.float32)


def backward_kernel(place, x_ref, gain, bias, w_in, w_out, w_pde, own, received, hidden_ref, silu_ref, slope_ref, updated_ref, send, keep, d_x_ref, mirrored_ref):
    base, core = place[0], place[1]
    for s in range(4):
        for b in range(8):
            mirrored_ref[pl.ds((8 * s + b) * 8, 8), :] = received[base + s, pl.ds(b, 8, stride=8), :]
    mine, mirrored = own[...], mirrored_ref[...]
    lane = lax.broadcasted_iota(jnp.int32, (PAIRS, C), 1)
    lane_float = lane.astype(jnp.float32)
    scored = mine[:, MASK : MASK + 1]
    onehot = lane_float == mine[:, LABEL : LABEL + 1]
    onehot_mirrored = lane_float == mirrored[:, LABEL : LABEL + 1]
    scores = mine + mirrored
    highest = jnp.max(jnp.where(lane < BINS, scores, -jnp.inf), axis=1, keepdims=True)
    shifted = jnp.where(lane < BINS, jnp.exp(jnp.minimum(scores - highest, 0.0)), 0.0)
    total = jnp.sum(shifted, axis=1, keepdims=True)
    picked = jnp.sum(jnp.where(onehot, scores, 0.0), axis=1, keepdims=True)
    loss = jnp.sum(scored * (highest + jnp.log(total) - picked))
    count = jnp.sum(scored)
    labelled = jnp.where(onehot, 1.0, 0.0) + jnp.where(onehot_mirrored, 1.0, 0.0)
    d_sym = scored * (2.0 * (shifted / total) - labelled)
    d_sym = split(d_sym)

    x = x_ref[...]
    scale, unit, normed = norm(x, gain[...], bias[...])
    d_updated = dot(d_sym, split(padded(w_pde[...])), 1, 1)
    d_pde = dot(split(updated_ref[...]), d_sym, 0, 0)
    d_updated_split = split(d_updated)
    d_out = dot(split(hidden_ref[...]), d_updated_split, 0, 0)
    d_hidden = dot(d_updated_split, split(w_out[...]), 1, 1)
    d_in_gate = split(d_hidden * slope_ref[...])
    d_in_up = split(d_hidden * silu_ref[...])
    normed = split(normed)
    d_gate = dot(d_in_gate, normed, 0, 0)
    d_up = dot(d_in_up, normed, 0, 0)
    weights = w_in[...]
    d_normed = dot(d_in_gate, split(weights[:H]), 1, 0) + dot(d_in_up, split(weights[H:]), 1, 0)
    d_unit = d_normed * gain[...]
    d_x_ref[...] = d_updated + scale * (
        d_unit - jnp.mean(d_unit, axis=1, keepdims=True) - unit * jnp.mean(d_unit * unit, axis=1, keepdims=True)
    )

    sub = lax.broadcasted_iota(jnp.int32, (8, C), 0)
    first = core == 0

    def put(rows, lows, highs):
        keep[pl.ds(rows, 8), :] = jnp.where(first, lows, highs)
        send[pl.ds(rows, 8), :] = jnp.where(first, highs, lows)

    for yl, d_half in ((0, d_gate), (1, d_up)):
        for xx in range(4):
            for yh in range(2):
                start = ((yl * 4 + xx) * 2 + yh) * BIG
                for m in range(4):
                    one = (xx * 8 + 2 * m) * 16 + yh * 8
                    even, odd = d_half[one : one + 8], d_half[one + 16 : one + 24]
                    lows = jnp.where(sub < 4, even, pltpu.roll(odd, 4, 0))
                    highs = jnp.where(sub < 4, pltpu.roll(even, 4, 0), odd)
                    put(start + 8 * m, lows, highs)
                for half in range(2):
                    halves = []
                    for cc in range(2):
                        tile = None
                        for low in range(4):
                            one = ((yl * 4 + xx) * 8 + 4 * half + low) * 8
                            shift = (2 * low - 4 * yh - 2 * cc) % 8
                            piece = d_out[one : one + 8]
                            piece = pltpu.roll(piece, shift, 0) if shift else piece
                            tile = piece if low == 0 else jnp.where(sub < 2 * low, tile, piece)
                        halves.append(tile)
                    put(start + 32 + 8 * half, *halves)
    packed = [d_pde[64 * k : 64 * k + 32] + pltpu.roll(d_pde[64 * k + 32 : 64 * k + 64], 64, 1) for k in range(2)]
    for k in range(4):
        put(16 * BIG + 8 * k, packed[0][8 * k : 8 * k + 8], packed[1][8 * k : 8 * k + 8])
    d_gain = jnp.sum(d_normed * unit, axis=0, keepdims=True)
    d_bias = jnp.sum(d_normed, axis=0, keepdims=True)
    lane = lax.broadcasted_iota(jnp.int32, (8, C), 1)
    tail = jnp.where(sub == 0, d_gain, jnp.where(sub == 1, d_bias, 0.0))
    tail = jnp.where((sub == 2) & (lane == 0), loss, tail)
    tail = jnp.where((sub == 2) & (lane == 1), count, tail)
    put(16 * BIG + 32, tail, tail)


def core_sum_kernel(keep, received, send):
    total = keep[...] + received[...]
    for d in range(16):
        send[d, 0:BIG, :] = total[d * BIG : (d + 1) * BIG]
        send[d, BIG : BIG + SMALL, :] = total[16 * BIG :]


def plane_sum_kernel(received, send):
    total = received[0]
    for d in range(1, 16):
        total = total + received[d]
    for z in range(8):
        send[z, 0:4, :] = total[4 * z : 4 * z + 4]
        send[z, 4:6, :] = total[32 + 2 * z : 34 + 2 * z]
        send[z, 6:8, :] = jnp.zeros((2, C), jnp.float32)
        send[z, 8 : 8 + SMALL, :] = total[BIG:]


def column_sum_kernel(received, d_x, loss, d_x_out, d_gain, d_bias, d_in, d_out, d_pde):
    total = received[0]
    for d in range(1, 8):
        total = total + received[d]
    tail = total[40:48]
    count = tail[2:3, 1:2]
    inverse = 1.0 / count
    loss[...] = tail[2:3, 0:1] / count
    d_in[...] = total[0:4] * inverse
    d_out[...] = total[4:6] * inverse
    d_pde[...] = total[8:40] * inverse
    d_gain[...] = tail[0:1] * inverse
    d_bias[...] = tail[1:2] * inverse
    d_x_out[...] = d_x[...] * inverse


def join_kernel(place, mine, other, out):
    core = place[1]
    for who, value in ((core, mine[...]), (1 - core, other[...])):
        out[pl.ds(64 * who, 32), :] = value[:, :BINS]
        out[pl.ds(64 * who + 32, 32), :] = pltpu.roll(value, 64, 1)[:, :BINS]


VMEM = pl.BlockSpec(memory_space=pltpu.VMEM)
SMEM = pl.BlockSpec(memory_space=pltpu.SMEM)


def call(kernel, outs, in_specs, scratch=(), name=None):
    shapes = [jax.ShapeDtypeStruct(shape, jnp.float32) for shape in outs]
    return pl.pallas_call(
        kernel,
        out_shape=shapes,
        in_specs=in_specs,
        out_specs=[VMEM] * len(outs),
        scratch_shapes=list(scratch),
        compiler_params=pltpu.CompilerParams(vmem_limit_bytes=48 << 20),
        name=name,
    )


def mirror_groups():
    groups, diagonal = [], []
    for q in range(8):
        for r in range(q + 1, 8):
            groups.append([q * 32 + 4 * r + u for u in range(4)] + [r * 32 + 4 * q + u for u in range(4)])
        diagonal.append([q * 36 + u for u in range(4)])
    return groups + [diagonal[k] + diagonal[k + 1] for k in range(0, 8, 2)]


def on_device(pair_rep, ln_gain, ln_bias, w_in, w_out, w_pde, labels, pair_mask):
    row, z, core = lax.axis_index(ROW), lax.axis_index("z"), lax.axis_index("co")
    base = jnp.where((row < z) | ((row == z) & (row % 2 == 1)), 4, 0)
    place = jnp.stack([base, core]).astype(jnp.int32)
    x = pair_rep.reshape(PAIRS, C)
    gain, bias = ln_gain.reshape(1, C), ln_bias.reshape(1, C)
    send, own, hidden, silu, slope, updated = call(
        forward_kernel,
        [(8, 64, C), (PAIRS, C), (PAIRS, H), (PAIRS, H), (PAIRS, H), (PAIRS, C)],
        [SMEM] + [VMEM] * 8,
        name="forward",
    )(place, x, gain, bias, w_in, w_out, w_pde, labels, pair_mask)
    received = lax.all_to_all(send, AXES, 0, 0, axis_index_groups=mirror_groups(), tiled=True)
    slab = (16 * BIG + SMALL, C)
    send, keep, d_x = call(
        backward_kernel,
        [slab, slab, (PAIRS, C)],
        [SMEM] + [VMEM] * 12,
        scratch=[pltpu.VMEM((PAIRS, C), jnp.float32)],
        name="backward",
    )(place, x, gain, bias, w_in, w_out, w_pde, own, received, hidden, silu, slope, updated)
    other_core = [(0, 1), (1, 0)]
    received = lax.ppermute(send, "co", other_core)
    (send,) = call(core_sum_kernel, [(16, BIG + SMALL, C)], [VMEM] * 2, name="core_sum")(keep, received)
    received = lax.all_to_all(send, PLANE, 0, 0, tiled=True)
    (send,) = call(plane_sum_kernel, [(8, 8 + SMALL, C)], [VMEM], name="plane_sum")(received)
    received = lax.all_to_all(send, "z", 0, 0, tiled=True)
    loss, d_x, d_gain, d_bias, d_in, d_out, d_pde = call(
        column_sum_kernel,
        [(1, 1), (PAIRS, C), (1, C), (1, C), (4, C), (2, C), (32, C)],
        [VMEM] * 2,
        name="column_sum",
    )(received, d_x)
    other = lax.ppermute(d_pde, "co", other_core)
    (d_pde,) = call(join_kernel, [(C, BINS)], [SMEM] + [VMEM] * 2, name="join")(place, d_pde, other)
    return (
        loss.reshape(()),
        d_x.reshape(ROWS, COLS, C),
        d_gain.reshape(C),
        d_bias.reshape(C),
        d_in,
        d_out,
        d_pde,
    )


def solution(mesh):
    torus = Mesh(mesh.devices.reshape(2, 4, 8, 2, 2), AXES)
    return jax.shard_map(
        on_device,
        mesh=torus,
        in_specs=(P(ROW, COL, None), P(), P(), P(), P(), P(), P(ROW, COL), P(ROW, COL)),
        out_specs=(P(), P(ROW, COL, None), P(), P(), P(ROW + COL, None), P(ROW + COL, None), P()),
        check_vma=False,
    )
```

```python
import functools

import jax
import jax.numpy as jnp
from jax import lax
from jax.experimental import pallas as pl
from jax.experimental.pallas import tpu as pltpu
from jax.sharding import Mesh
from jax.sharding import PartitionSpec as P

AXES = ("yl", "x", "z", "yh", "co")
ROW = ("yl", "x")
COL = ("z", "yh", "co")
PLANE = ("yl", "x", "yh")

EPSILON = 1e-05
ROWS, COLS, C, H, BINS = 32, 8, 128, 512, 64
PAIRS = ROWS * COLS
F32, BF16 = jnp.float32, jnp.bfloat16
LAST = BINS - 1
MASK = BINS
BIG = 40
SMALL = 40
SLAB = 16 * BIG + SMALL


def split(value):
    high = value.astype(jnp.bfloat16)
    return high, (value - high.astype(jnp.float32)).astype(jnp.bfloat16)


def dot(left, right, left_dim, right_dim):
    dims = (((left_dim,), (right_dim,)), ((), ()))
    one = functools.partial(lax.dot_general, dimension_numbers=dims, preferred_element_type=jnp.float32)
    return one(left[0], right[0]) + (one(left[0], right[1]) + one(left[1], right[0]))


def norm(x):
    centred = x - jnp.mean(x, axis=-1, keepdims=True)
    scale = lax.rsqrt(jnp.mean(centred * centred, axis=-1, keepdims=True) + EPSILON)
    return scale, centred * scale


def forward_kernel(
    place, x_hbm, gain_hbm, bias_hbm, w_in_hbm, w_out_hbm, w_pde_hbm, labels_hbm, mask_hbm,
    send, own, gain, w_pde, updated_high, updated_low, unit_ref, scale_ref, normed_high, normed_low,
    in_high, in_low, out_high, out_low, silu_ref, slope_ref, hidden_high, hidden_low,
    x_ref, bias, w_in, w_out, labels, mask, sems,
):
    ins = (x_hbm, gain_hbm, bias_hbm, labels_hbm, mask_hbm, w_in_hbm, w_out_hbm, w_pde_hbm)
    refs = (x_ref, gain, bias, labels, mask, w_in, w_out, w_pde)
    copies = [pltpu.make_async_copy(i, r, sems.at[k]) for k, (i, r) in enumerate(zip(ins, refs))]
    for copy in copies:
        copy.start()
    base = place[0]
    for s in range(4):
        send[4 - base + s] = jnp.zeros((32, C), F32)
    for k in range(3):
        copies[k].wait()
    x = x_ref[...]
    scale, unit = norm(x)
    unit_ref[...] = unit
    scale_ref[...] = jnp.broadcast_to(scale, (PAIRS, C))
    normed = split(unit * gain[...] + bias[...])
    normed_high[...], normed_low[...] = normed
    copies[3].wait()
    copies[4].wait()
    code = (labels[...] + 64 * mask[...]).astype(F32).astype(BF16)
    pair = lax.broadcasted_iota(jnp.int32, (PAIRS, ROWS), 0)
    row = lax.broadcasted_iota(jnp.int32, (PAIRS, ROWS), 1)
    spread = jnp.where(pair // COLS == row, 1.0, 0.0).astype(BF16)
    by_row = lax.dot_general(spread, code, (((1,), (1,)), ((), ())), preferred_element_type=F32)
    pair = lax.broadcasted_iota(jnp.int32, (PAIRS, COLS), 0)
    col = lax.broadcasted_iota(jnp.int32, (PAIRS, COLS), 1)
    code = jnp.sum(jnp.where(pair % COLS == col, by_row, 0.0), axis=1, keepdims=True)
    scored = jnp.where(code >= 64.0, 1.0, 0.0)
    copies[5].wait()
    weights = split(w_in[...])
    in_high[...], in_low[...] = weights
    projected_in = dot(normed, weights, 1, 1)
    gate, up = projected_in[:, :H], projected_in[:, H:]
    sigmoid = 1.0 / (1.0 + jnp.exp(-gate))
    silu = gate * sigmoid
    silu_ref[...] = silu
    slope_ref[...] = up * (sigmoid * (1.0 + gate * (1.0 - sigmoid)))
    hidden = split(silu * up)
    hidden_high[...], hidden_low[...] = hidden
    copies[6].wait()
    weights = split(w_out[...])
    out_high[...], out_low[...] = weights
    updated = split(x + dot(hidden, weights, 1, 0))
    updated_high[...], updated_low[...] = updated
    copies[7].wait()
    weights = jnp.concatenate([w_pde[...], jnp.zeros((C - BINS, C), F32)], axis=0)
    projected = dot(updated, split(weights), 1, 1)
    lane = lax.broadcasted_iota(jnp.int32, (PAIRS, C), 1)
    projected = projected - projected[:, LAST:BINS]
    projected = jnp.where(lane < LAST, projected, jnp.where(lane == LAST, code - 64.0 * scored, scored))
    own[...] = projected
    low = lane[:32] < BINS
    for s in range(4):
        one = projected[64 * s : 64 * s + 32]
        two = projected[64 * s + 32 : 64 * s + 64]
        send[base + s] = jnp.where(low, one, pltpu.roll(two, BINS, 1))


def backward_kernel(
    place, received, own, gain, w_pde, updated_high, updated_low, unit_ref, scale_ref, normed_high, normed_low,
    in_high, in_low, out_high, out_low, silu_ref, slope_ref, hidden_high, hidden_low,
    send, keep, d_x_ref, flat_ref, mirrored_ref,
):
    base, core = place[0], place[1]
    for s in range(4):
        block = received[base + s]
        flat_ref[64 * s : 64 * s + 32, :] = block
        flat_ref[64 * s + 32 : 64 * s + 64, :] = pltpu.roll(block, BINS, 1)
    for s in range(4):
        for b in range(8):
            mirrored_ref[(8 * s + b) * 8 : (8 * s + b) * 8 + 8, :] = flat_ref[pl.ds(64 * s + b, 8, stride=8), :]
    mine, mirrored = own[...], mirrored_ref[...]
    lane = lax.broadcasted_iota(jnp.int32, (PAIRS, C), 1)
    lane_float = lane.astype(jnp.float32)
    scored = mine[:, MASK : MASK + 1]
    onehot = lane_float == mine[:, LAST:BINS]
    onehot_mirrored = lane_float == mirrored[:, LAST:BINS]
    scores = jnp.where(lane < LAST, mine + mirrored, jnp.where(lane == LAST, 0.0, -jnp.inf))
    highest = jnp.max(scores, axis=1, keepdims=True)
    shifted = jnp.exp(scores - highest)
    total = jnp.sum(shifted, axis=1, keepdims=True)
    picked = jnp.sum(jnp.where(onehot, scores, 0.0), axis=1, keepdims=True)
    loss = jnp.sum(scored * (highest + jnp.log(total) - picked))
    count = jnp.sum(scored)
    labelled = jnp.where(onehot, 1.0, 0.0) + jnp.where(onehot_mirrored, 1.0, 0.0)
    d_sym = split(scored * (shifted * (2.0 / total) - labelled))
    narrow = tuple(part[:, :BINS] for part in d_sym)

    d_updated = dot(narrow, split(w_pde[...]), 1, 0)
    d_pde = dot(narrow, (updated_high[...], updated_low[...]), 0, 0)
    d_out = dot((hidden_high[...], hidden_low[...]), d_sym, 0, 0)
    d_hidden = dot(split(d_updated), (out_high[...], out_low[...]), 1, 1)
    d_in_gate = split(d_hidden * slope_ref[...])
    d_in_up = split(d_hidden * silu_ref[...])
    normed = normed_high[...], normed_low[...]
    d_gate = dot(d_in_gate, normed, 0, 0)
    d_up = dot(d_in_up, normed, 0, 0)
    d_normed = dot(d_in_gate, (in_high[:H], in_low[:H]), 1, 0) + dot(d_in_up, (in_high[H:], in_low[H:]), 1, 0)
    unit = unit_ref[...]
    d_unit = d_normed * gain[...]
    d_x_ref[...] = d_updated + scale_ref[...] * (
        d_unit - jnp.mean(d_unit, axis=1, keepdims=True) - unit * jnp.mean(d_unit * unit, axis=1, keepdims=True)
    )

    sub = lax.broadcasted_iota(jnp.int32, (8, C), 0)
    lane = lax.broadcasted_iota(jnp.int32, (8, C), 1)
    first = core == 0

    def put(rows, lows, highs):
        keep[rows : rows + 8, :] = jnp.where(first, lows, highs)
        send[rows : rows + 8, :] = jnp.where(first, highs, lows)

    for yl, d_half in ((0, d_gate), (1, d_up)):
        for xx in range(4):
            for yh in range(2):
                start = ((yl * 4 + xx) * 2 + yh) * BIG
                for m in range(4):
                    one = (xx * 8 + 2 * m) * 16 + yh * 8
                    even, odd = d_half[one : one + 8], d_half[one + 16 : one + 24]
                    lows = jnp.where(sub < 4, even, pltpu.roll(odd, 4, 0))
                    highs = jnp.where(sub < 4, pltpu.roll(even, 4, 0), odd)
                    put(start + 8 * m, lows, highs)
                cores = []
                for cc in range(2):
                    halves = []
                    for half in range(2):
                        tile = None
                        for low in range(4):
                            one = ((yl * 4 + xx) * 8 + 4 * half + low) * 8
                            shift = (2 * low - 4 * yh - 2 * cc) % 8
                            piece = d_out[one : one + 8]
                            piece = pltpu.roll(piece, shift, 0) if shift else piece
                            tile = piece if low == 0 else jnp.where(sub < 2 * low, tile, piece)
                        halves.append(tile)
                    cores.append(jnp.where(lane < BINS, halves[0], pltpu.roll(halves[1], BINS, 1)))
                put(start + 32, *cores)
    for k in range(4):
        put(16 * BIG + 8 * k, d_pde[8 * k : 8 * k + 8], d_pde[32 + 8 * k : 40 + 8 * k])
    d_gain = jnp.sum(d_normed * unit, axis=0, keepdims=True)
    d_bias = jnp.sum(d_normed, axis=0, keepdims=True)
    tail = jnp.where(sub == 0, d_gain, jnp.where(sub == 1, d_bias, 0.0))
    tail = jnp.where((sub == 2) & (lane == 0), loss, tail)
    tail = jnp.where((sub == 2) & (lane == 1), count, tail)
    put(16 * BIG + 32, tail, tail)


def core_sum_kernel(keep, received, send):
    total = keep[...] + received[...]
    for d in range(16):
        send[d, 0:BIG, :] = total[d * BIG : (d + 1) * BIG]
        send[d, BIG : BIG + SMALL, :] = total[16 * BIG :]


def plane_sum_kernel(received, send):
    total = received[0]
    for d in range(1, 16):
        total = total + received[d]
    tail = total[BIG + 32 : BIG + 35]
    lane = lax.broadcasted_iota(jnp.int32, (2, C), 1)
    measures = pltpu.roll(jnp.broadcast_to(tail[2:3], (8, C)), BINS, 1)[0:2]
    for z in range(8):
        send[z, 0:4, :] = total[4 * z : 4 * z + 4]
        pair = total[32 + 2 * (z % 4) : 34 + 2 * (z % 4)]
        pair = pltpu.roll(jnp.concatenate([pair] * 4, axis=0), BINS, 1)[0:2] if z >= 4 else pair
        send[z, 4:6, :] = jnp.where(lane < BINS, pair, measures)
        send[z, 6:8, :] = tail[0:2]
        send[z, 8:40, :] = total[BIG : BIG + 32]


def column_sum_kernel(received, w_pde, d_x, d_pde, loss, d_gain, d_bias, d_in, d_out, d_x_out):
    total = received[0]
    for d in range(1, 8):
        total = total + received[d]
    count = total[4:5, BINS + 1 : BINS + 2]
    inverse = 1.0 / count
    loss[...] = total[4:5, BINS : BINS + 1] / count
    d_pde[...] = total[8:40] * inverse
    d_in[...] = total[0:4] * inverse
    d_gain[...] = total[6:7] * inverse
    d_bias[...] = total[7:8] * inverse
    scores_part = split(total[0:8][:, :BINS])
    d_out[...] = dot(scores_part, split(w_pde[...]), 1, 0)[4:6] * inverse
    d_x_out[...] = d_x[...] * inverse


def join_kernel(place, mine, other, out):
    core = place[1]
    first = core == 0
    out[0:32, :] = jnp.where(first, mine[...], other[...])
    out[32:64, :] = jnp.where(first, other[...], mine[...])


VMEM = pl.BlockSpec(memory_space=pltpu.VMEM)
SMEM = pl.BlockSpec(memory_space=pltpu.SMEM)
HBM = pl.BlockSpec(memory_space=pltpu.HBM)


def call(kernel, outs, in_specs, scratch=(), name=None, limit=12):
    outs = [out if isinstance(out[0], tuple) else (out, F32) for out in outs]
    shapes = [jax.ShapeDtypeStruct(*out) for out in outs]
    return pl.pallas_call(
        kernel,
        out_shape=shapes,
        in_specs=in_specs,
        out_specs=[VMEM] * len(outs),
        scratch_shapes=list(scratch),
        compiler_params=pltpu.CompilerParams(vmem_limit_bytes=limit << 20),
        name=name,
    )


def mirror_groups():
    groups, diagonal = [], []
    for q in range(8):
        for r in range(q + 1, 8):
            groups.append([q * 32 + 4 * r + u for u in range(4)] + [r * 32 + 4 * q + u for u in range(4)])
        diagonal.append([q * 36 + u for u in range(4)])
    return groups + [diagonal[k] + diagonal[k + 1] for k in range(0, 8, 2)]


def on_device(pair_rep, ln_gain, ln_bias, w_in, w_out, w_pde, labels, pair_mask):
    row, z, core = lax.axis_index(ROW), lax.axis_index("z"), lax.axis_index("co")
    base = jnp.where((row < z) | ((row == z) & (row % 2 == 1)), 4, 0)
    place = jnp.stack([base, core]).astype(jnp.int32)
    x = pair_rep.reshape(PAIRS, C)
    gain, bias, w_pde = ln_gain.reshape(1, C), ln_bias.reshape(1, C), w_pde.T
    wide, half = (PAIRS, C), (PAIRS, H)
    send, *kept = call(
        forward_kernel,
        [(8, 32, C), wide, (1, C), (BINS, C), (wide, BF16), (wide, BF16), wide, wide, (wide, BF16), (wide, BF16)]
        + [((2 * H, C), BF16)] * 2
        + [((H, C), BF16)] * 2
        + [half, half, (half, BF16), (half, BF16)],
        [SMEM] + [HBM] * 8,
        scratch=[
            pltpu.VMEM(wide, F32),
            pltpu.VMEM((1, C), F32),
            pltpu.VMEM((2 * H, C), F32),
            pltpu.VMEM((H, C), F32),
            pltpu.VMEM((COLS, ROWS), jnp.int32),
            pltpu.VMEM((COLS, ROWS), jnp.int32),
            pltpu.SemaphoreType.DMA((8,)),
        ],
        name="forward",
    )(place, *(pltpu.with_memory_space_constraint(a, pltpu.HBM) for a in (x, gain, bias, w_in, w_out, w_pde, labels.T, pair_mask.T)))
    received = lax.all_to_all(send, AXES, 0, 0, axis_index_groups=mirror_groups(), tiled=True)
    send, keep, d_x = call(
        backward_kernel,
        [(SLAB, C), (SLAB, C), wide],
        [SMEM] + [VMEM] * 18,
        scratch=[pltpu.VMEM(wide, F32)] * 2,
        name="backward",
    )(place, received, *kept)
    other_core = [(0, 1), (1, 0)]
    received = lax.ppermute(send, "co", other_core)
    (send,) = call(core_sum_kernel, [(16, BIG + SMALL, C)], [VMEM] * 2, name="core_sum")(keep, received)
    received = lax.all_to_all(send, PLANE, 0, 0, tiled=True)
    (send,) = call(plane_sum_kernel, [(8, 40, C)], [VMEM], name="plane_sum")(received)
    received = lax.all_to_all(send, "z", 0, 0, tiled=True)
    d_pde, loss, d_gain, d_bias, d_in, d_out, d_x = call(
        column_sum_kernel,
        [(32, C), (1, 1), (1, C), (1, C), (4, C), (2, C), wide],
        [VMEM] * 3,
        name="column_sum",
    )(received, kept[2], d_x)
    other = lax.ppermute(d_pde, "co", other_core)
    (d_pde,) = call(join_kernel, [(BINS, C)], [SMEM] + [VMEM] * 2, name="join")(place, d_pde, other)
    return (
        loss.reshape(()),
        d_x.reshape(ROWS, COLS, C),
        d_gain.reshape(C),
        d_bias.reshape(C),
        d_in,
        d_out,
        d_pde.T,
    )


def solution(mesh):
    torus = Mesh(mesh.devices.reshape(2, 4, 8, 2, 2), AXES)
    return jax.shard_map(
        on_device,
        mesh=torus,
        in_specs=(P(ROW, COL, None), P(), P(), P(), P(), P(), P(ROW, COL), P(ROW, COL)),
        out_specs=(P(), P(ROW, COL, None), P(), P(), P(ROW + COL, None), P(ROW + COL, None), P()),
        check_vma=False,
    )
```

```python
import functools

import jax
import jax.numpy as jnp
from jax import lax
from jax.experimental import pallas as pl
from jax.experimental.pallas import tpu as pltpu
from jax.sharding import Mesh
from jax.sharding import PartitionSpec as P

AXES = ("yl", "x", "z", "yh", "co")
ROW = ("yl", "x")
COL = ("z", "yh", "co")
PLANE = ("yl", "x", "yh")

EPSILON = 1e-05
ROWS, COLS, C, H, BINS = 32, 8, 128, 512, 64
PAIRS = ROWS * COLS
F32, BF16 = jnp.float32, jnp.bfloat16
LAST = BINS - 1
MASK = BINS
BIG = 40
SMALL = 40
SLAB = 16 * BIG + SMALL


def split(value):
    high = value.astype(jnp.bfloat16)
    return high, (value - high.astype(jnp.float32)).astype(jnp.bfloat16)


def product(left, right, left_dim, right_dim):
    dims = (((left_dim,), (right_dim,)), ((), ()))
    return lax.dot_general(left, right, dims, preferred_element_type=F32)


def wide(left, right, left_dim, right_dim):
    both = product(left[0], jnp.concatenate(right, axis=1 - right_dim), left_dim, right_dim)
    return both[:, :C] + (both[:, C:] + product(left[1], right[0], left_dim, right_dim))


def deep(left, right, right_dim):
    stacked = product(jnp.concatenate(left, axis=1), jnp.concatenate([right[0]] * 2, axis=right_dim), 1, right_dim)
    return stacked + product(left[0], right[1], 1, right_dim)


def norm(x):
    centred = x - jnp.mean(x, axis=-1, keepdims=True)
    scale = lax.rsqrt(jnp.mean(centred * centred, axis=-1, keepdims=True) + EPSILON)
    return scale, centred * scale


def mirror_base():
    row, z = lax.axis_index("yl") * 4 + lax.axis_index("x"), lax.axis_index("z")
    return jnp.where((row < z) | ((row == z) & (row % 2 == 1)), 4, 0)


def forward_kernel(
    x_hbm, gain_hbm, bias_hbm, w_in_hbm, w_out_hbm, w_pde_hbm, labels_hbm, mask_hbm,
    send, own, gain, w_pde, updated_high, updated_low, unit_ref, scale_ref, normed_high, normed_low,
    in_high, in_low, out_high, out_low, silu_ref, slope_ref, hidden_high, hidden_low,
    x_ref, bias, w_in, w_out, labels, mask, sems,
):
    ins = (x_hbm, gain_hbm, bias_hbm, labels_hbm, mask_hbm, w_in_hbm, w_out_hbm, w_pde_hbm)
    refs = (x_ref, gain, bias, labels, mask, w_in, w_out, w_pde)
    copies = [pltpu.make_async_copy(i, r, sems.at[k]) for k, (i, r) in enumerate(zip(ins, refs))]
    for copy in copies:
        copy.start()
    base = mirror_base()
    for s in range(4):
        send[4 - base + s] = jnp.zeros((32, C), F32)
    for k in range(3):
        copies[k].wait()
    x = x_ref[...]
    scale, unit = norm(x)
    unit_ref[...] = unit
    scale_ref[...] = jnp.broadcast_to(scale, (PAIRS, C))
    normed = split(unit * gain[...] + bias[...])
    normed_high[...], normed_low[...] = normed
    copies[3].wait()
    copies[4].wait()
    code = (labels[...] + 64 * mask[...]).astype(F32).astype(BF16)
    pair = lax.broadcasted_iota(jnp.int32, (PAIRS, ROWS), 0)
    row = lax.broadcasted_iota(jnp.int32, (PAIRS, ROWS), 1)
    spread = jnp.where(pair // COLS == row, 1.0, 0.0).astype(BF16)
    by_row = lax.dot_general(spread, code, (((1,), (1,)), ((), ())), preferred_element_type=F32)
    pair = lax.broadcasted_iota(jnp.int32, (PAIRS, COLS), 0)
    col = lax.broadcasted_iota(jnp.int32, (PAIRS, COLS), 1)
    code = jnp.sum(jnp.where(pair % COLS == col, by_row, 0.0), axis=1, keepdims=True)
    scored = jnp.where(code >= 64.0, 1.0, 0.0)
    copies[5].wait()
    weights = split(w_in[...])
    in_high[...], in_low[...] = weights
    projected_in = deep(normed, weights, 1)
    gate, up = projected_in[:, :H], projected_in[:, H:]
    sigmoid = 1.0 / (1.0 + jnp.exp(-gate))
    silu = gate * sigmoid
    silu_ref[...] = silu
    slope_ref[...] = up * (sigmoid * (1.0 + gate * (1.0 - sigmoid)))
    hidden = split(silu * up)
    hidden_high[...], hidden_low[...] = hidden
    copies[6].wait()
    weights = split(w_out[...])
    out_high[...], out_low[...] = weights
    updated = split(x + wide(hidden, weights, 1, 0))
    updated_high[...], updated_low[...] = updated
    copies[7].wait()
    high, low = split(w_pde[...])
    weights = jnp.concatenate(
        [jnp.concatenate([high, high], axis=1), jnp.concatenate([low, jnp.zeros_like(low)], axis=1)], axis=0
    )
    projected = product(jnp.concatenate(updated, axis=1), weights, 1, 1)
    projected = projected + pltpu.roll(projected, BINS, 1)
    lane = lax.broadcasted_iota(jnp.int32, (PAIRS, C), 1)
    projected = projected - projected[:, LAST:BINS]
    projected = jnp.where(lane < LAST, projected, jnp.where(lane == LAST, code - 64.0 * scored, scored))
    own[...] = projected
    low = lane[:32] < BINS
    for s in range(4):
        one = projected[64 * s : 64 * s + 32]
        two = projected[64 * s + 32 : 64 * s + 64]
        send[base + s] = jnp.where(low, one, pltpu.roll(two, BINS, 1))


def backward_kernel(
    received, own, gain, w_pde, updated_high, updated_low, unit_ref, scale_ref, normed_high, normed_low,
    in_high, in_low, out_high, out_low, silu_ref, slope_ref, hidden_high, hidden_low,
    send, keep, d_x_ref, flat_ref, mirrored_ref,
):
    base, core = mirror_base(), lax.axis_index("co")
    for s in range(4):
        block = received[base + s]
        flat_ref[64 * s : 64 * s + 32, :] = block
        flat_ref[64 * s + 32 : 64 * s + 64, :] = pltpu.roll(block, BINS, 1)
    for s in range(4):
        for b in range(8):
            mirrored_ref[(8 * s + b) * 8 : (8 * s + b) * 8 + 8, :] = flat_ref[pl.ds(64 * s + b, 8, stride=8), :]
    mine, mirrored = own[...], mirrored_ref[...]
    lane = lax.broadcasted_iota(jnp.int32, (PAIRS, C), 1)
    lane_float = lane.astype(jnp.float32)
    scored = mine[:, MASK : MASK + 1]
    onehot = lane_float == mine[:, LAST:BINS]
    onehot_mirrored = lane_float == mirrored[:, LAST:BINS]
    scores = jnp.where(lane < LAST, mine + mirrored, jnp.where(lane == LAST, 0.0, -jnp.inf))
    highest = jnp.max(scores, axis=1, keepdims=True)
    shifted = jnp.exp(scores - highest)
    total = jnp.sum(shifted, axis=1, keepdims=True)
    picked = jnp.sum(jnp.where(onehot, scores, 0.0), axis=1, keepdims=True)
    loss = jnp.sum(scored * (highest + jnp.log(total) - picked))
    count = jnp.sum(scored)
    labelled = jnp.where(onehot, 1.0, 0.0) + jnp.where(onehot_mirrored, 1.0, 0.0)
    d_sym = scored * (shifted * (2.0 / total) - labelled)
    high = d_sym.astype(BF16)
    rest = d_sym - high.astype(F32)
    packed = jnp.where(lane < BINS, high.astype(F32), pltpu.roll(rest, BINS, 1)).astype(BF16)

    high_pde, low_pde = split(w_pde[...])
    weights = jnp.concatenate([high_pde, high_pde, low_pde, jnp.zeros_like(low_pde)], axis=0)
    d_updated = product(jnp.concatenate([packed, high], axis=1), weights, 1, 0)
    d_pde = product(packed, jnp.concatenate([updated_high[...], updated_low[...]], axis=1), 0, 0)
    d_pde = d_pde[:BINS, :C] + (d_pde[:BINS, C:] + d_pde[BINS:, :C])
    d_out = product(hidden_high[...], packed, 0, 0)
    d_out = d_out + (pltpu.roll(d_out, BINS, 1) + product(hidden_low[...], high, 0, 0))
    d_hidden = deep(split(d_updated), (out_high[...], out_low[...]), 1)
    d_in_gate = split(d_hidden * slope_ref[...])
    d_in_up = split(d_hidden * silu_ref[...])
    normed = normed_high[...], normed_low[...]
    d_gate = wide(d_in_gate, normed, 0, 0)
    d_up = wide(d_in_up, normed, 0, 0)
    d_normed = wide(d_in_gate, (in_high[:H], in_low[:H]), 1, 0) + wide(d_in_up, (in_high[H:], in_low[H:]), 1, 0)
    unit = unit_ref[...]
    d_unit = d_normed * gain[...]
    d_x_ref[...] = d_updated + scale_ref[...] * (
        d_unit - jnp.mean(d_unit, axis=1, keepdims=True) - unit * jnp.mean(d_unit * unit, axis=1, keepdims=True)
    )

    sub = lax.broadcasted_iota(jnp.int32, (8, C), 0)
    lane = lax.broadcasted_iota(jnp.int32, (8, C), 1)
    first = core == 0

    def put(rows, lows, highs):
        keep[rows : rows + 8, :] = jnp.where(first, lows, highs)
        send[rows : rows + 8, :] = jnp.where(first, highs, lows)

    for yl, d_half in ((0, d_gate), (1, d_up)):
        for xx in range(4):
            for yh in range(2):
                start = ((yl * 4 + xx) * 2 + yh) * BIG
                for m in range(4):
                    one = (xx * 8 + 2 * m) * 16 + yh * 8
                    even, odd = d_half[one : one + 8], d_half[one + 16 : one + 24]
                    lows = jnp.where(sub < 4, even, pltpu.roll(odd, 4, 0))
                    highs = jnp.where(sub < 4, pltpu.roll(even, 4, 0), odd)
                    put(start + 8 * m, lows, highs)
                cores = []
                for cc in range(2):
                    halves = []
                    for half in range(2):
                        tile = None
                        for low in range(4):
                            one = ((yl * 4 + xx) * 8 + 4 * half + low) * 8
                            shift = (2 * low - 4 * yh - 2 * cc) % 8
                            piece = d_out[one : one + 8]
                            piece = pltpu.roll(piece, shift, 0) if shift else piece
                            tile = piece if low == 0 else jnp.where(sub < 2 * low, tile, piece)
                        halves.append(tile)
                    cores.append(jnp.where(lane < BINS, halves[0], pltpu.roll(halves[1], BINS, 1)))
                put(start + 32, *cores)
    for k in range(4):
        put(16 * BIG + 8 * k, d_pde[8 * k : 8 * k + 8], d_pde[32 + 8 * k : 40 + 8 * k])
    d_gain = jnp.sum(d_normed * unit, axis=0, keepdims=True)
    d_bias = jnp.sum(d_normed, axis=0, keepdims=True)
    tail = jnp.where(sub == 0, d_gain, jnp.where(sub == 1, d_bias, 0.0))
    tail = jnp.where((sub == 2) & (lane == 0), loss, tail)
    tail = jnp.where((sub == 2) & (lane == 1), count, tail)
    put(16 * BIG + 32, tail, tail)


def core_sum_kernel(keep, received, send):
    total = keep[...] + received[...]
    for d in range(16):
        send[d, 0:BIG, :] = total[d * BIG : (d + 1) * BIG]
        send[d, BIG : BIG + SMALL, :] = total[16 * BIG :]


def plane_sum_kernel(received, send):
    total = received[0]
    for d in range(1, 16):
        total = total + received[d]
    tail = total[BIG + 32 : BIG + 35]
    lane = lax.broadcasted_iota(jnp.int32, (2, C), 1)
    measures = pltpu.roll(jnp.broadcast_to(tail[2:3], (8, C)), BINS, 1)[0:2]
    for z in range(8):
        send[z, 0:4, :] = total[4 * z : 4 * z + 4]
        pair = total[32 + 2 * (z % 4) : 34 + 2 * (z % 4)]
        pair = pltpu.roll(jnp.concatenate([pair] * 4, axis=0), BINS, 1)[0:2] if z >= 4 else pair
        send[z, 4:6, :] = jnp.where(lane < BINS, pair, measures)
        send[z, 6:8, :] = tail[0:2]
        send[z, 8:40, :] = total[BIG : BIG + 32]


def pde_sum_kernel(received, d_pde):
    total = received[0]
    for d in range(1, 8):
        total = total + received[d]
    d_pde[...] = total[8:40] * (1.0 / total[4:5, BINS + 1 : BINS + 2])


def column_sum_kernel(received, w_pde, d_x, loss, d_gain, d_bias, d_in, d_out, d_x_out):
    total = received[0, 0:8]
    for d in range(1, 8):
        total = total + received[d, 0:8]
    count = total[4:5, BINS + 1 : BINS + 2]
    inverse = 1.0 / count
    loss[...] = total[4:5, BINS : BINS + 1] / count
    d_in[...] = total[0:4] * inverse
    d_gain[...] = total[6:7] * inverse
    d_bias[...] = total[7:8] * inverse
    left, right = split(total[:, :BINS]), split(w_pde[...])
    projected = product(left[0], right[0], 1, 0) + (product(left[0], right[1], 1, 0) + product(left[1], right[0], 1, 0))
    d_out[...] = projected[4:6] * inverse
    d_x_out[...] = d_x[...] * inverse


def join_kernel(mine, other, out):
    first = lax.axis_index("co") == 0
    out[0:32, :] = jnp.where(first, mine[...], other[...])
    out[32:64, :] = jnp.where(first, other[...], mine[...])


VMEM = pl.BlockSpec(memory_space=pltpu.VMEM)
HBM = pl.BlockSpec(memory_space=pltpu.HBM)


def call(kernel, outs, in_specs, scratch=(), name=None, limit=12):
    outs = [out if isinstance(out[0], tuple) else (out, F32) for out in outs]
    shapes = [jax.ShapeDtypeStruct(*out) for out in outs]
    return pl.pallas_call(
        kernel,
        out_shape=shapes,
        in_specs=in_specs,
        out_specs=[VMEM] * len(outs),
        scratch_shapes=list(scratch),
        compiler_params=pltpu.CompilerParams(vmem_limit_bytes=limit << 20),
        name=name,
    )


def mirror_groups():
    groups, diagonal = [], []
    for q in range(8):
        for r in range(q + 1, 8):
            groups.append([q * 32 + 4 * r + u for u in range(4)] + [r * 32 + 4 * q + u for u in range(4)])
        diagonal.append([q * 36 + u for u in range(4)])
    return groups + [diagonal[k] + diagonal[k + 1] for k in range(0, 8, 2)]


def on_device(pair_rep, ln_gain, ln_bias, w_in, w_out, w_pde, labels, pair_mask):
    x = pair_rep.reshape(PAIRS, C)
    gain, bias, w_pde = ln_gain.reshape(1, C), ln_bias.reshape(1, C), w_pde.T
    full, half = (PAIRS, C), (PAIRS, H)
    send, *kept = call(
        forward_kernel,
        [(8, 32, C), full, (1, C), (BINS, C), (full, BF16), (full, BF16), full, full, (full, BF16), (full, BF16)]
        + [((2 * H, C), BF16)] * 2
        + [((H, C), BF16)] * 2
        + [half, half, (half, BF16), (half, BF16)],
        [HBM] * 8,
        scratch=[
            pltpu.VMEM(full, F32),
            pltpu.VMEM((1, C), F32),
            pltpu.VMEM((2 * H, C), F32),
            pltpu.VMEM((H, C), F32),
            pltpu.VMEM((COLS, ROWS), jnp.int32),
            pltpu.VMEM((COLS, ROWS), jnp.int32),
            pltpu.SemaphoreType.DMA((8,)),
        ],
        name="forward",
    )(*(pltpu.with_memory_space_constraint(a, pltpu.HBM) for a in (x, gain, bias, w_in, w_out, w_pde, labels.T, pair_mask.T)))
    received = lax.all_to_all(send, AXES, 0, 0, axis_index_groups=mirror_groups(), tiled=True)
    send, keep, d_x = call(
        backward_kernel,
        [(SLAB, C), (SLAB, C), full],
        [VMEM] * 18,
        scratch=[pltpu.VMEM(full, F32)] * 2,
        name="backward",
    )(received, *kept)
    other_core = [(0, 1), (1, 0)]
    received = lax.ppermute(send, "co", other_core)
    (send,) = call(core_sum_kernel, [(16, BIG + SMALL, C)], [VMEM] * 2, name="core_sum")(keep, received)
    received = lax.all_to_all(send, PLANE, 0, 0, tiled=True)
    (send,) = call(plane_sum_kernel, [(8, 40, C)], [VMEM], name="plane_sum")(received)
    received = lax.all_to_all(send, "z", 0, 0, tiled=True)
    (d_pde,) = call(pde_sum_kernel, [(32, C)], [VMEM], name="pde_sum")(received)
    other = lax.ppermute(d_pde, "co", other_core)
    loss, d_gain, d_bias, d_in, d_out, d_x = call(
        column_sum_kernel,
        [(1, 1), (1, C), (1, C), (4, C), (2, C), full],
        [VMEM] * 3,
        name="column_sum",
    )(received, kept[2], d_x)
    (d_pde,) = call(join_kernel, [(BINS, C)], [VMEM] * 2, name="join")(d_pde, other)
    return (
        loss.reshape(()),
        d_x.reshape(ROWS, COLS, C),
        d_gain.reshape(C),
        d_bias.reshape(C),
        d_in,
        d_out,
        d_pde.T,
    )


def solution(mesh):
    torus = Mesh(mesh.devices.reshape(2, 4, 8, 2, 2), AXES)
    return jax.shard_map(
        on_device,
        mesh=torus,
        in_specs=(P(ROW, COL, None), P(), P(), P(), P(), P(), P(ROW, COL), P(ROW, COL)),
        out_specs=(P(), P(ROW, COL, None), P(), P(), P(ROW + COL, None), P(ROW + COL, None), P()),
        check_vma=False,
    )
```

```python
import functools

import jax
import jax.numpy as jnp
from jax import lax
from jax.experimental import pallas as pl
from jax.experimental.pallas import tpu as pltpu
from jax.sharding import Mesh
from jax.sharding import PartitionSpec as P

AXES = ("yl", "x", "z", "yh", "co")
ROW = ("yl", "x")
COL = ("z", "yh", "co")
PLANE = ("yl", "x", "yh")

EPSILON = 1e-05
ROWS, COLS, C, H, BINS = 32, 8, 128, 512, 64
PAIRS = ROWS * COLS
HALF = PAIRS // 2
F32, BF16 = jnp.float32, jnp.bfloat16
LAST = BINS - 1
MASK = BINS
BIG = 40
SMALL = 40
SLAB = 16 * BIG + SMALL


def split(value):
    high = value.astype(jnp.bfloat16)
    return high, (value - high.astype(jnp.float32)).astype(jnp.bfloat16)


def product(left, right, left_dim, right_dim):
    dims = (((left_dim,), (right_dim,)), ((), ()))
    return lax.dot_general(left, right, dims, preferred_element_type=F32)


def wide(left, right, left_dim, right_dim):
    both = product(left[0], jnp.concatenate(right, axis=1 - right_dim), left_dim, right_dim)
    return both[:, :C] + (both[:, C:] + product(left[1], right[0], left_dim, right_dim))


def deep(left, right, right_dim):
    stacked = product(jnp.concatenate(left, axis=1), jnp.concatenate([right[0]] * 2, axis=right_dim), 1, right_dim)
    return stacked + product(left[0], right[1], 1, right_dim)


def norm(x):
    centred = x - jnp.mean(x, axis=-1, keepdims=True)
    scale = lax.rsqrt(jnp.mean(centred * centred, axis=-1, keepdims=True) + EPSILON)
    return scale, centred * scale


def weights_kernel(w_in_hbm, w_out_hbm, in_high, in_low, out_high, out_low, w_in, w_out, sems):
    copies = [pltpu.make_async_copy(w_in_hbm, w_in, sems.at[0]), pltpu.make_async_copy(w_out_hbm, w_out, sems.at[1])]
    for copy in copies:
        copy.start()
    copies[0].wait()
    in_high[...], in_low[...] = split(w_in[...])
    copies[1].wait()
    out_high[...], out_low[...] = split(w_out[...])


def forward_kernel(
    x_hbm, x_other, labels_other, mask_other, in_high, in_low, out_high, out_low,
    gain_hbm, bias_hbm, w_pde_hbm, labels_hbm, mask_hbm,
    send, own, gain, w_pde, updated_high, updated_low, unit_ref, scale_ref, normed_high, normed_low,
    silu_ref, slope_ref, hidden_high, hidden_low,
    x_ref, bias, labels, mask, sems,
):
    core = lax.axis_index("co")
    first = core == 0
    rows = pl.ds(pl.multiple_of(core * HALF, HALF), HALF)
    ins = (x_hbm.at[rows, :], gain_hbm, bias_hbm, labels_hbm, mask_hbm, w_pde_hbm)
    refs = (x_ref, gain, bias, labels, mask, w_pde)
    copies = [pltpu.make_async_copy(i, r, sems.at[k]) for k, (i, r) in enumerate(zip(ins, refs))]
    for copy in copies:
        copy.start()
    copies[0].wait()
    mine, other = x_ref[...], x_other[rows, :]
    x = jnp.concatenate([jnp.where(first, mine, other), jnp.where(first, other, mine)], axis=0)
    scale, unit = norm(x)
    unit_ref[...] = unit
    scale_ref[...] = jnp.broadcast_to(scale, (PAIRS, C))
    for k in range(1, 6):
        copies[k].wait()
    normed = split(unit * gain[...] + bias[...])
    normed_high[...], normed_low[...] = normed
    mine = (labels[...] + 64 * mask[...]).astype(F32)
    other = (labels_other[...] + 64 * mask_other[...]).astype(F32)
    pair = lax.broadcasted_iota(jnp.int32, (HALF, ROWS), 0)
    row = lax.broadcasted_iota(jnp.int32, (HALF, ROWS), 1)
    spread = jnp.where(pair // COLS + 16 * core == row, 1.0, 0.0).astype(BF16)
    codes = (jnp.where(first, mine, other), jnp.where(first, other, mine))
    by_row = jnp.concatenate([product(spread, code.astype(BF16), 1, 1) for code in codes], axis=0)
    pair = lax.broadcasted_iota(jnp.int32, (PAIRS, COLS), 0)
    col = lax.broadcasted_iota(jnp.int32, (PAIRS, COLS), 1)
    code = jnp.sum(jnp.where(pair % COLS == col, by_row, 0.0), axis=1, keepdims=True)
    scored = jnp.where(code >= 64.0, 1.0, 0.0)
    projected_in = deep(normed, (in_high[...], in_low[...]), 1)
    gate, up = projected_in[:, :H], projected_in[:, H:]
    sigmoid = 1.0 / (1.0 + jnp.exp(-gate))
    silu = gate * sigmoid
    silu_ref[...] = silu
    slope_ref[...] = up * (sigmoid * (1.0 + gate * (1.0 - sigmoid)))
    hidden = split(silu * up)
    hidden_high[...], hidden_low[...] = hidden
    updated = split(x + wide(hidden, (out_high[...], out_low[...]), 1, 0))
    updated_high[...], updated_low[...] = updated
    high, low = split(w_pde[...])
    weights = jnp.concatenate(
        [jnp.concatenate([high, high], axis=1), jnp.concatenate([low, jnp.zeros_like(low)], axis=1)], axis=0
    )
    projected = product(jnp.concatenate(updated, axis=1), weights, 1, 1)
    projected = projected + pltpu.roll(projected, BINS, 1)
    lane = lax.broadcasted_iota(jnp.int32, (PAIRS, C), 1)
    projected = projected - projected[:, LAST:BINS]
    projected = jnp.where(lane < LAST, projected, jnp.where(lane == LAST, code - 64.0 * scored, scored))
    own[...] = projected
    send[...] = jnp.where(lane[:HALF] < BINS, projected[:HALF], pltpu.roll(projected[HALF:], BINS, 1))


def backward_kernel(
    received, in_high, in_low, out_high, out_low, own, gain, w_pde, updated_high, updated_low, unit_ref, scale_ref,
    normed_high, normed_low, silu_ref, slope_ref, hidden_high, hidden_low,
    send, keep, d_x_ref, flat_ref, mirrored_ref,
):
    core = lax.axis_index("co")
    first = core == 0
    flat_ref[0:HALF, :] = received[...]
    flat_ref[HALF:PAIRS, :] = pltpu.roll(received[...], BINS, 1)
    for half in range(2):
        for row in range(16):
            start = HALF * (row // 8) + 64 * half + row % 8
            mirrored_ref[HALF * half + 8 * row : HALF * half + 8 * row + 8, :] = flat_ref[pl.ds(start, 8, stride=8), :]
    mine, mirrored = own[...], mirrored_ref[...]
    lane = lax.broadcasted_iota(jnp.int32, (PAIRS, C), 1)
    lane_float = lane.astype(jnp.float32)
    scored = mine[:, MASK : MASK + 1]
    onehot = lane_float == mine[:, LAST:BINS]
    onehot_mirrored = lane_float == mirrored[:, LAST:BINS]
    scores = jnp.where(lane < LAST, mine + mirrored, jnp.where(lane == LAST, 0.0, -jnp.inf))
    highest = jnp.max(scores, axis=1, keepdims=True)
    shifted = jnp.exp(scores - highest)
    total = jnp.sum(shifted, axis=1, keepdims=True)
    picked = jnp.sum(jnp.where(onehot, scores, 0.0), axis=1, keepdims=True)
    loss = jnp.sum(scored * (highest + jnp.log(total) - picked))
    count = jnp.sum(scored)
    labelled = jnp.where(onehot, 1.0, 0.0) + jnp.where(onehot_mirrored, 1.0, 0.0)
    d_sym = scored * (shifted * (2.0 / total) - labelled)
    high = d_sym.astype(BF16)
    rest = d_sym - high.astype(F32)
    packed = jnp.where(lane < BINS, high.astype(F32), pltpu.roll(rest, BINS, 1)).astype(BF16)

    high_pde, low_pde = split(w_pde[...])
    weights = jnp.concatenate([high_pde, high_pde, low_pde, jnp.zeros_like(low_pde)], axis=0)
    d_updated = product(jnp.concatenate([packed, high], axis=1), weights, 1, 0)
    d_pde = product(packed, jnp.concatenate([updated_high[...], updated_low[...]], axis=1), 0, 0)
    d_pde = d_pde[:BINS, :C] + (d_pde[:BINS, C:] + d_pde[BINS:, :C])
    d_out = product(hidden_high[...], packed, 0, 0)
    d_out = d_out + (pltpu.roll(d_out, BINS, 1) + product(hidden_low[...], high, 0, 0))
    d_hidden = deep(split(d_updated), (out_high[...], out_low[...]), 1)
    d_in_gate = split(d_hidden * slope_ref[...])
    d_in_up = split(d_hidden * silu_ref[...])
    normed = normed_high[...], normed_low[...]
    d_gate = wide(d_in_gate, normed, 0, 0)
    d_up = wide(d_in_up, normed, 0, 0)
    d_normed = wide(d_in_gate, (in_high[:H], in_low[:H]), 1, 0) + wide(d_in_up, (in_high[H:], in_low[H:]), 1, 0)
    unit = unit_ref[...]
    d_unit = d_normed * gain[...]
    d_x = d_updated + scale_ref[...] * (
        d_unit - jnp.mean(d_unit, axis=1, keepdims=True) - unit * jnp.mean(d_unit * unit, axis=1, keepdims=True)
    )

    sub = lax.broadcasted_iota(jnp.int32, (8, C), 0)
    lane = lax.broadcasted_iota(jnp.int32, (8, C), 1)
    d_x_ref[...] = jnp.where(first, d_x[:HALF], d_x[HALF:])
    send[SLAB : SLAB + HALF, :] = jnp.where(first, d_x[HALF:], d_x[:HALF])

    def put(rows, lows, highs):
        keep[rows : rows + 8, :] = jnp.where(first, lows, highs)
        send[rows : rows + 8, :] = jnp.where(first, highs, lows)

    for yl, d_half in ((0, d_gate), (1, d_up)):
        for xx in range(4):
            for yh in range(2):
                start = ((yl * 4 + xx) * 2 + yh) * BIG
                for m in range(4):
                    one = (xx * 8 + 2 * m) * 16 + yh * 8
                    even, odd = d_half[one : one + 8], d_half[one + 16 : one + 24]
                    lows = jnp.where(sub < 4, even, pltpu.roll(odd, 4, 0))
                    highs = jnp.where(sub < 4, pltpu.roll(even, 4, 0), odd)
                    put(start + 8 * m, lows, highs)
                cores = []
                for cc in range(2):
                    halves = []
                    for half in range(2):
                        tile = None
                        for low in range(4):
                            one = ((yl * 4 + xx) * 8 + 4 * half + low) * 8
                            shift = (2 * low - 4 * yh - 2 * cc) % 8
                            piece = d_out[one : one + 8]
                            piece = pltpu.roll(piece, shift, 0) if shift else piece
                            tile = piece if low == 0 else jnp.where(sub < 2 * low, tile, piece)
                        halves.append(tile)
                    cores.append(jnp.where(lane < BINS, halves[0], pltpu.roll(halves[1], BINS, 1)))
                put(start + 32, *cores)
    for k in range(4):
        put(16 * BIG + 8 * k, d_pde[8 * k : 8 * k + 8], d_pde[32 + 8 * k : 40 + 8 * k])
    d_gain = jnp.sum(d_normed * unit, axis=0, keepdims=True)
    d_bias = jnp.sum(d_normed, axis=0, keepdims=True)
    tail = jnp.where(sub == 0, d_gain, jnp.where(sub == 1, d_bias, 0.0))
    tail = jnp.where((sub == 2) & (lane == 0), loss, tail)
    tail = jnp.where((sub == 2) & (lane == 1), count, tail)
    put(16 * BIG + 32, tail, tail)


def core_sum_kernel(keep, received, send):
    total = keep[...] + received[0:SLAB]
    for d in range(16):
        send[d, 0:BIG, :] = total[d * BIG : (d + 1) * BIG]
        send[d, BIG : BIG + SMALL, :] = total[16 * BIG :]


def plane_sum_kernel(received, send):
    total = received[0]
    for d in range(1, 16):
        total = total + received[d]
    tail = total[BIG + 32 : BIG + 35]
    lane = lax.broadcasted_iota(jnp.int32, (2, C), 1)
    measures = pltpu.roll(jnp.broadcast_to(tail[2:3], (8, C)), BINS, 1)[0:2]
    for z in range(8):
        send[z, 0:4, :] = total[4 * z : 4 * z + 4]
        pair = total[32 + 2 * (z % 4) : 34 + 2 * (z % 4)]
        pair = pltpu.roll(jnp.concatenate([pair] * 4, axis=0), BINS, 1)[0:2] if z >= 4 else pair
        send[z, 4:6, :] = jnp.where(lane < BINS, pair, measures)
        send[z, 6:8, :] = tail[0:2]
        send[z, 8:40, :] = total[BIG : BIG + 32]


def pde_sum_kernel(received, d_pde):
    total = received[0]
    for d in range(1, 8):
        total = total + received[d]
    d_pde[...] = total[8:40] * (1.0 / total[4:5, BINS + 1 : BINS + 2])


def column_sum_kernel(received, w_pde, d_x, d_x_other, loss, d_gain, d_bias, d_in, d_out, d_x_out):
    total = received[0, 0:8]
    for d in range(1, 8):
        total = total + received[d, 0:8]
    count = total[4:5, BINS + 1 : BINS + 2]
    inverse = 1.0 / count
    loss[...] = total[4:5, BINS : BINS + 1] / count
    d_in[...] = total[0:4] * inverse
    d_gain[...] = total[6:7] * inverse
    d_bias[...] = total[7:8] * inverse
    left, right = split(total[:, :BINS]), split(w_pde[...])
    projected = product(left[0], right[0], 1, 0) + (product(left[0], right[1], 1, 0) + product(left[1], right[0], 1, 0))
    d_out[...] = projected[4:6] * inverse
    first = lax.axis_index("co") == 0
    mine, other = d_x[...] * inverse, d_x_other[SLAB : SLAB + HALF] * inverse
    d_x_out[0:HALF, :] = jnp.where(first, mine, other)
    d_x_out[HALF:PAIRS, :] = jnp.where(first, other, mine)


def join_kernel(mine, other, out):
    first = lax.axis_index("co") == 0
    out[0:32, :] = jnp.where(first, mine[...], other[...])
    out[32:64, :] = jnp.where(first, other[...], mine[...])


VMEM = pl.BlockSpec(memory_space=pltpu.VMEM)
HBM = pl.BlockSpec(memory_space=pltpu.HBM)


def call(kernel, outs, in_specs, scratch=(), name=None, limit=12):
    outs = [out if isinstance(out[0], tuple) else (out, F32) for out in outs]
    shapes = [jax.ShapeDtypeStruct(*out) for out in outs]
    return pl.pallas_call(
        kernel,
        out_shape=shapes,
        in_specs=in_specs,
        out_specs=[VMEM] * len(outs),
        scratch_shapes=list(scratch),
        compiler_params=pltpu.CompilerParams(vmem_limit_bytes=limit << 20),
        name=name,
    )


def mirror_pairs():
    return [
        (r * 32 + z * 4 + yh * 2 + co, z * 32 + r * 4 + co * 2 + yh)
        for r in range(8)
        for z in range(8)
        for yh in range(2)
        for co in range(2)
    ]


def on_device(pair_rep, ln_gain, ln_bias, w_in, w_out, w_pde, labels, pair_mask):
    swap = [(0, 1), (1, 0)]
    x = pair_rep.reshape(PAIRS, C)
    gain, bias, w_pde, labels, mask = ln_gain.reshape(1, C), ln_bias.reshape(1, C), w_pde.T, labels.T, pair_mask.T
    x_other, labels_other, mask_other = (lax.ppermute(a, "co", swap) for a in (x, labels, mask))
    full, half = (PAIRS, C), (PAIRS, H)
    in_hbm = functools.partial(pltpu.with_memory_space_constraint, memory_space=pltpu.HBM)
    weights = call(
        weights_kernel,
        [((2 * H, C), BF16)] * 2 + [((H, C), BF16)] * 2,
        [HBM] * 2,
        scratch=[pltpu.VMEM((2 * H, C), F32), pltpu.VMEM((H, C), F32), pltpu.SemaphoreType.DMA((2,))],
        name="weights",
    )(in_hbm(w_in), in_hbm(w_out))
    send, *kept = call(
        forward_kernel,
        [(HALF, C), full, (1, C), (BINS, C), (full, BF16), (full, BF16), full, full, (full, BF16), (full, BF16)]
        + [half, half, (half, BF16), (half, BF16)],
        [HBM] + [VMEM] * 7 + [HBM] * 5,
        scratch=[
            pltpu.VMEM((HALF, C), F32),
            pltpu.VMEM((1, C), F32),
            pltpu.VMEM((COLS, ROWS), jnp.int32),
            pltpu.VMEM((COLS, ROWS), jnp.int32),
            pltpu.SemaphoreType.DMA((6,)),
        ],
        name="forward",
    )(in_hbm(x), x_other, labels_other, mask_other, *weights, *(in_hbm(a) for a in (gain, bias, w_pde, labels, mask)))
    received = lax.ppermute(send, AXES, mirror_pairs())
    send, keep, d_x = call(
        backward_kernel,
        [(SLAB + HALF, C), (SLAB, C), (HALF, C)],
        [VMEM] * 18,
        scratch=[pltpu.VMEM(full, F32)] * 2,
        name="backward",
    )(received, *weights, *kept)
    from_core = lax.ppermute(send, "co", swap)
    (send,) = call(core_sum_kernel, [(16, BIG + SMALL, C)], [VMEM] * 2, name="core_sum")(keep, from_core)
    received = lax.all_to_all(send, PLANE, 0, 0, tiled=True)
    (send,) = call(plane_sum_kernel, [(8, 40, C)], [VMEM], name="plane_sum")(received)
    received = lax.all_to_all(send, "z", 0, 0, tiled=True)
    (d_pde,) = call(pde_sum_kernel, [(32, C)], [VMEM], name="pde_sum")(received)
    other = lax.ppermute(d_pde, "co", swap)
    loss, d_gain, d_bias, d_in, d_out, d_x = call(
        column_sum_kernel,
        [(1, 1), (1, C), (1, C), (4, C), (2, C), full],
        [VMEM] * 4,
        name="column_sum",
    )(received, kept[2], d_x, from_core)
    (d_pde,) = call(join_kernel, [(BINS, C)], [VMEM] * 2, name="join")(d_pde, other)
    return (
        loss.reshape(()),
        d_x.reshape(ROWS, COLS, C),
        d_gain.reshape(C),
        d_bias.reshape(C),
        d_in,
        d_out,
        d_pde.T,
    )


def solution(mesh):
    torus = Mesh(mesh.devices.reshape(2, 4, 8, 2, 2), AXES)
    return jax.shard_map(
        on_device,
        mesh=torus,
        in_specs=(P(ROW, COL, None), P(), P(), P(), P(), P(), P(ROW, COL), P(ROW, COL)),
        out_specs=(P(), P(ROW, COL, None), P(), P(), P(ROW + COL, None), P(ROW + COL, None), P()),
        check_vma=False,
    )
```

```python
import functools

import jax
import jax.numpy as jnp
from jax import lax
from jax.experimental import pallas as pl
from jax.experimental.pallas import tpu as pltpu
from jax.sharding import Mesh
from jax.sharding import PartitionSpec as P

AXES = ("yl", "x", "z", "yh", "co")
ROW = ("yl", "x")
COL = ("z", "yh", "co")
PLANE = ("yl", "x", "yh")

EPSILON = 1e-05
ROWS, COLS, C, H, BINS = 32, 8, 128, 512, 64
PAIRS = ROWS * COLS
HALF = PAIRS // 2
F32, BF16 = jnp.float32, jnp.bfloat16
LAST = BINS - 1
MASK = BINS
BIG = 40
SMALL = 40
SLAB = 16 * BIG + SMALL


def split(value):
    high = value.astype(jnp.bfloat16)
    return high, (value - high.astype(jnp.float32)).astype(jnp.bfloat16)


def product(left, right, left_dim, right_dim):
    dims = (((left_dim,), (right_dim,)), ((), ()))
    return lax.dot_general(left, right, dims, preferred_element_type=F32)


def wide(left, right, left_dim, right_dim):
    both = product(left[0], jnp.concatenate(right, axis=1 - right_dim), left_dim, right_dim)
    return both[:, :C] + (both[:, C:] + product(left[1], right[0], left_dim, right_dim))


def deep(left, right, right_dim):
    stacked = product(jnp.concatenate(left, axis=1), jnp.concatenate([right[0]] * 2, axis=right_dim), 1, right_dim)
    return stacked + product(left[0], right[1], 1, right_dim)


def norm(x):
    centred = x - jnp.mean(x, axis=-1, keepdims=True)
    scale = lax.rsqrt(jnp.mean(centred * centred, axis=-1, keepdims=True) + EPSILON)
    return scale, centred * scale


def load_kernel(
    x_hbm, gain_hbm, bias_hbm, labels_hbm, mask_hbm, w_pde_hbm, w_in_hbm, w_out_hbm,
    x_ref, gain, bias, labels, mask, w_pde, in_high, in_low, out_high, out_low, w_in, w_out, sems,
):
    rows = pl.ds(pl.multiple_of(lax.axis_index("co") * HALF, HALF), HALF)
    ins = (w_in_hbm, w_out_hbm, x_hbm.at[rows, :], gain_hbm, bias_hbm, labels_hbm, mask_hbm, w_pde_hbm)
    refs = (w_in, w_out, x_ref, gain, bias, labels, mask, w_pde)
    copies = [pltpu.make_async_copy(i, r, sems.at[k]) for k, (i, r) in enumerate(zip(ins, refs))]
    for copy in copies:
        copy.start()
    copies[0].wait()
    in_high[...], in_low[...] = split(w_in[...])
    copies[1].wait()
    out_high[...], out_low[...] = split(w_out[...])
    for copy in copies[2:]:
        copy.wait()


def forward_kernel(
    x_other, labels_other, mask_other, x_ref, gain, bias, labels, mask, w_pde, in_high, in_low, out_high, out_low,
    send, own, updated_high, updated_low, unit_ref, scale_ref, normed_high, normed_low,
    silu_ref, slope_ref, hidden_high, hidden_low,
):
    core = lax.axis_index("co")
    first = core == 0
    rows = pl.ds(pl.multiple_of(core * HALF, HALF), HALF)
    mine, other = x_ref[...], x_other[rows, :]
    x = jnp.concatenate([jnp.where(first, mine, other), jnp.where(first, other, mine)], axis=0)
    scale, unit = norm(x)
    unit_ref[...] = unit
    scale_ref[...] = jnp.broadcast_to(scale, (PAIRS, C))
    normed = split(unit * gain[...] + bias[...])
    normed_high[...], normed_low[...] = normed
    mine = (labels[...] + 64 * mask[...]).astype(F32)
    other = (labels_other[...] + 64 * mask_other[...]).astype(F32)
    pair = lax.broadcasted_iota(jnp.int32, (HALF, ROWS), 0)
    row = lax.broadcasted_iota(jnp.int32, (HALF, ROWS), 1)
    spread = jnp.where(pair // COLS + 16 * core == row, 1.0, 0.0).astype(BF16)
    codes = (jnp.where(first, mine, other), jnp.where(first, other, mine))
    by_row = jnp.concatenate([product(spread, code.astype(BF16), 1, 1) for code in codes], axis=0)
    pair = lax.broadcasted_iota(jnp.int32, (PAIRS, COLS), 0)
    col = lax.broadcasted_iota(jnp.int32, (PAIRS, COLS), 1)
    code = jnp.sum(jnp.where(pair % COLS == col, by_row, 0.0), axis=1, keepdims=True)
    scored = jnp.where(code >= 64.0, 1.0, 0.0)
    projected_in = deep(normed, (in_high[...], in_low[...]), 1)
    gate, up = projected_in[:, :H], projected_in[:, H:]
    sigmoid = 1.0 / (1.0 + jnp.exp(-gate))
    silu = gate * sigmoid
    silu_ref[...] = silu
    slope_ref[...] = up * (sigmoid * (1.0 + gate * (1.0 - sigmoid)))
    hidden = split(silu * up)
    hidden_high[...], hidden_low[...] = hidden
    updated = split(x + wide(hidden, (out_high[...], out_low[...]), 1, 0))
    updated_high[...], updated_low[...] = updated
    high, low = split(w_pde[...])
    weights = jnp.concatenate(
        [jnp.concatenate([high, high], axis=1), jnp.concatenate([low, jnp.zeros_like(low)], axis=1)], axis=0
    )
    projected = product(jnp.concatenate(updated, axis=1), weights, 1, 1)
    projected = projected + pltpu.roll(projected, BINS, 1)
    lane = lax.broadcasted_iota(jnp.int32, (PAIRS, C), 1)
    projected = projected - projected[:, LAST:BINS]
    projected = jnp.where(lane < LAST, projected, jnp.where(lane == LAST, code - 64.0 * scored, scored))
    own[...] = projected
    send[...] = jnp.where(lane[:HALF] < BINS, projected[:HALF], pltpu.roll(projected[HALF:], BINS, 1))


def backward_kernel(
    received, gain, w_pde, in_high, in_low, out_high, out_low, own, updated_high, updated_low, unit_ref, scale_ref,
    normed_high, normed_low, silu_ref, slope_ref, hidden_high, hidden_low,
    send, keep, d_x_ref, flat_ref, mirrored_ref,
):
    core = lax.axis_index("co")
    first = core == 0
    flat_ref[0:HALF, :] = received[...]
    flat_ref[HALF:PAIRS, :] = pltpu.roll(received[...], BINS, 1)
    for half in range(2):
        for row in range(16):
            start = HALF * (row // 8) + 64 * half + row % 8
            mirrored_ref[HALF * half + 8 * row : HALF * half + 8 * row + 8, :] = flat_ref[pl.ds(start, 8, stride=8), :]
    mine, mirrored = own[...], mirrored_ref[...]
    lane = lax.broadcasted_iota(jnp.int32, (PAIRS, C), 1)
    lane_float = lane.astype(jnp.float32)
    scored = mine[:, MASK : MASK + 1]
    onehot = lane_float == mine[:, LAST:BINS]
    onehot_mirrored = lane_float == mirrored[:, LAST:BINS]
    scores = jnp.where(lane < LAST, mine + mirrored, jnp.where(lane == LAST, 0.0, -jnp.inf))
    highest = jnp.max(scores, axis=1, keepdims=True)
    shifted = jnp.exp(scores - highest)
    total = jnp.sum(shifted, axis=1, keepdims=True)
    picked = jnp.sum(jnp.where(onehot, scores, 0.0), axis=1, keepdims=True)
    loss = jnp.sum(scored * (highest + jnp.log(total) - picked))
    count = jnp.sum(scored)
    labelled = jnp.where(onehot, 1.0, 0.0) + jnp.where(onehot_mirrored, 1.0, 0.0)
    d_sym = scored * (shifted * (2.0 / total) - labelled)
    high = d_sym.astype(BF16)
    rest = d_sym - high.astype(F32)
    packed = jnp.where(lane < BINS, high.astype(F32), pltpu.roll(rest, BINS, 1)).astype(BF16)

    high_pde, low_pde = split(w_pde[...])
    weights = jnp.concatenate([high_pde, high_pde, low_pde, jnp.zeros_like(low_pde)], axis=0)
    d_updated = product(jnp.concatenate([packed, high], axis=1), weights, 1, 0)
    d_pde = product(packed, jnp.concatenate([updated_high[...], updated_low[...]], axis=1), 0, 0)
    d_pde = d_pde[:BINS, :C] + (d_pde[:BINS, C:] + d_pde[BINS:, :C])
    d_out = product(hidden_high[...], packed, 0, 0)
    d_out = d_out + (pltpu.roll(d_out, BINS, 1) + product(hidden_low[...], high, 0, 0))
    d_hidden = deep(split(d_updated), (out_high[...], out_low[...]), 1)
    d_in_gate = split(d_hidden * slope_ref[...])
    d_in_up = split(d_hidden * silu_ref[...])
    normed = normed_high[...], normed_low[...]
    d_gate = wide(d_in_gate, normed, 0, 0)
    d_up = wide(d_in_up, normed, 0, 0)
    d_normed = wide(d_in_gate, (in_high[:H], in_low[:H]), 1, 0) + wide(d_in_up, (in_high[H:], in_low[H:]), 1, 0)
    unit = unit_ref[...]
    d_unit = d_normed * gain[...]
    d_x = d_updated + scale_ref[...] * (
        d_unit - jnp.mean(d_unit, axis=1, keepdims=True) - unit * jnp.mean(d_unit * unit, axis=1, keepdims=True)
    )

    sub = lax.broadcasted_iota(jnp.int32, (8, C), 0)
    lane = lax.broadcasted_iota(jnp.int32, (8, C), 1)
    d_x_ref[...] = jnp.where(first, d_x[:HALF], d_x[HALF:])
    send[SLAB : SLAB + HALF, :] = jnp.where(first, d_x[HALF:], d_x[:HALF])

    def put(rows, lows, highs):
        keep[rows : rows + 8, :] = jnp.where(first, lows, highs)
        send[rows : rows + 8, :] = jnp.where(first, highs, lows)

    d_out_tiles = [
        [
            jnp.where(
                lane < BINS,
                d_out[(8 * k + low) * 8 : (8 * k + low) * 8 + 8],
                pltpu.roll(d_out[(8 * k + 4 + low) * 8 : (8 * k + 4 + low) * 8 + 8], BINS, 1),
            )
            for low in range(4)
        ]
        for k in range(8)
    ]
    for yl, d_half in ((0, d_gate), (1, d_up)):
        for xx in range(4):
            for yh in range(2):
                start = ((yl * 4 + xx) * 2 + yh) * BIG
                for m in range(4):
                    one = (xx * 8 + 2 * m) * 16 + yh * 8
                    even, odd = d_half[one : one + 8], d_half[one + 16 : one + 24]
                    lows = jnp.where(sub < 4, even, pltpu.roll(odd, 4, 0))
                    highs = jnp.where(sub < 4, pltpu.roll(even, 4, 0), odd)
                    put(start + 8 * m, lows, highs)
                cores = []
                for cc in range(2):
                    tile = None
                    for low, piece in enumerate(d_out_tiles[yl * 4 + xx]):
                        shift = (2 * low - 4 * yh - 2 * cc) % 8
                        piece = pltpu.roll(piece, shift, 0) if shift else piece
                        tile = piece if low == 0 else jnp.where(sub < 2 * low, tile, piece)
                    cores.append(tile)
                put(start + 32, *cores)
    for k in range(4):
        put(16 * BIG + 8 * k, d_pde[8 * k : 8 * k + 8], d_pde[32 + 8 * k : 40 + 8 * k])
    d_gain = jnp.sum(d_normed * unit, axis=0, keepdims=True)
    d_bias = jnp.sum(d_normed, axis=0, keepdims=True)
    tail = jnp.where(sub == 0, d_gain, jnp.where(sub == 1, d_bias, 0.0))
    tail = jnp.where((sub == 2) & (lane == 0), loss, tail)
    tail = jnp.where((sub == 2) & (lane == 1), count, tail)
    put(16 * BIG + 32, tail, tail)


def core_sum_kernel(keep, received, send):
    total = keep[...] + received[0:SLAB]
    for d in range(16):
        send[d, 0:BIG, :] = total[d * BIG : (d + 1) * BIG]
        send[d, BIG : BIG + SMALL, :] = total[16 * BIG :]


def plane_sum_kernel(received, send):
    total = received[0]
    for d in range(1, 16):
        total = total + received[d]
    tail = total[BIG + 32 : BIG + 35]
    lane = lax.broadcasted_iota(jnp.int32, (2, C), 1)
    measures = pltpu.roll(jnp.broadcast_to(tail[2:3], (8, C)), BINS, 1)[0:2]
    for z in range(8):
        send[z, 0:4, :] = total[4 * z : 4 * z + 4]
        pair = total[32 + 2 * (z % 4) : 34 + 2 * (z % 4)]
        pair = pltpu.roll(jnp.concatenate([pair] * 4, axis=0), BINS, 1)[0:2] if z >= 4 else pair
        send[z, 4:6, :] = jnp.where(lane < BINS, pair, measures)
        send[z, 6:8, :] = tail[0:2]
        send[z, 8:40, :] = total[BIG : BIG + 32]


def pde_sum_kernel(received, d_pde):
    total = received[0]
    for d in range(1, 8):
        total = total + received[d]
    d_pde[...] = total[8:40] * (1.0 / total[4:5, BINS + 1 : BINS + 2])


def column_sum_kernel(received, w_pde, d_x, d_x_other, loss, d_gain, d_bias, d_in, d_out, d_x_out):
    total = received[0, 0:8]
    for d in range(1, 8):
        total = total + received[d, 0:8]
    count = total[4:5, BINS + 1 : BINS + 2]
    inverse = 1.0 / count
    loss[...] = total[4:5, BINS : BINS + 1] / count
    d_in[...] = total[0:4] * inverse
    d_gain[...] = total[6:7] * inverse
    d_bias[...] = total[7:8] * inverse
    left, right = split(total[:, :BINS]), split(w_pde[...])
    projected = product(left[0], right[0], 1, 0) + (product(left[0], right[1], 1, 0) + product(left[1], right[0], 1, 0))
    d_out[...] = projected[4:6] * inverse
    first = lax.axis_index("co") == 0
    mine, other = d_x[...] * inverse, d_x_other[SLAB : SLAB + HALF] * inverse
    d_x_out[0:HALF, :] = jnp.where(first, mine, other)
    d_x_out[HALF:PAIRS, :] = jnp.where(first, other, mine)


def join_kernel(mine, other, out):
    first = lax.axis_index("co") == 0
    out[0:32, :] = jnp.where(first, mine[...], other[...])
    out[32:64, :] = jnp.where(first, other[...], mine[...])


VMEM = pl.BlockSpec(memory_space=pltpu.VMEM)
HBM = pl.BlockSpec(memory_space=pltpu.HBM)


def call(kernel, outs, in_specs, scratch=(), name=None, limit=12):
    outs = [out if isinstance(out[0], tuple) else (out, F32) for out in outs]
    shapes = [jax.ShapeDtypeStruct(*out) for out in outs]
    return pl.pallas_call(
        kernel,
        out_shape=shapes,
        in_specs=in_specs,
        out_specs=[VMEM] * len(outs),
        scratch_shapes=list(scratch),
        compiler_params=pltpu.CompilerParams(vmem_limit_bytes=limit << 20),
        name=name,
    )


def mirror_pairs():
    return [
        (r * 32 + z * 4 + yh * 2 + co, z * 32 + r * 4 + co * 2 + yh)
        for r in range(8)
        for z in range(8)
        for yh in range(2)
        for co in range(2)
    ]


def on_device(pair_rep, ln_gain, ln_bias, w_in, w_out, w_pde, labels, pair_mask):
    swap = [(0, 1), (1, 0)]
    x = pair_rep.reshape(PAIRS, C)
    gain, bias, w_pde, labels, mask = ln_gain.reshape(1, C), ln_bias.reshape(1, C), w_pde.T, labels.T, pair_mask.T
    x_other, labels_other, mask_other = (lax.ppermute(a, "co", swap) for a in (x, labels, mask))
    full, half = (PAIRS, C), (PAIRS, H)
    in_hbm = functools.partial(pltpu.with_memory_space_constraint, memory_space=pltpu.HBM)
    x, gain, bias, labels, mask, *weights = call(
        load_kernel,
        [(HALF, C), (1, C), (1, C), ((COLS, ROWS), jnp.int32), ((COLS, ROWS), jnp.int32), (BINS, C)]
        + [((2 * H, C), BF16)] * 2
        + [((H, C), BF16)] * 2,
        [HBM] * 8,
        scratch=[pltpu.VMEM((2 * H, C), F32), pltpu.VMEM((H, C), F32), pltpu.SemaphoreType.DMA((8,))],
        name="load",
    )(*(in_hbm(a) for a in (x, gain, bias, labels, mask, w_pde, w_in, w_out)))
    send, *kept = call(
        forward_kernel,
        [(HALF, C), full, (full, BF16), (full, BF16), full, full, (full, BF16), (full, BF16)]
        + [half, half, (half, BF16), (half, BF16)],
        [VMEM] * 13,
        name="forward",
    )(x_other, labels_other, mask_other, x, gain, bias, labels, mask, *weights)
    received = lax.ppermute(send, AXES, mirror_pairs())
    send, keep, d_x = call(
        backward_kernel,
        [(SLAB + HALF, C), (SLAB, C), (HALF, C)],
        [VMEM] * 18,
        scratch=[pltpu.VMEM(full, F32)] * 2,
        name="backward",
    )(received, gain, *weights, *kept)
    from_core = lax.ppermute(send, "co", swap)
    (send,) = call(core_sum_kernel, [(16, BIG + SMALL, C)], [VMEM] * 2, name="core_sum")(keep, from_core)
    received = lax.all_to_all(send, PLANE, 0, 0, tiled=True)
    (send,) = call(plane_sum_kernel, [(8, 40, C)], [VMEM], name="plane_sum")(received)
    received = lax.all_to_all(send, "z", 0, 0, tiled=True)
    (d_pde,) = call(pde_sum_kernel, [(32, C)], [VMEM], name="pde_sum")(received)
    other = lax.ppermute(d_pde, "co", swap)
    loss, d_gain, d_bias, d_in, d_out, d_x = call(
        column_sum_kernel,
        [(1, 1), (1, C), (1, C), (4, C), (2, C), full],
        [VMEM] * 4,
        name="column_sum",
    )(received, weights[0], d_x, from_core)
    (d_pde,) = call(join_kernel, [(BINS, C)], [VMEM] * 2, name="join")(d_pde, other)
    return (
        loss.reshape(()),
        d_x.reshape(ROWS, COLS, C),
        d_gain.reshape(C),
        d_bias.reshape(C),
        d_in,
        d_out,
        d_pde.T,
    )


def solution(mesh):
    torus = Mesh(mesh.devices.reshape(2, 4, 8, 2, 2), AXES)
    return jax.shard_map(
        on_device,
        mesh=torus,
        in_specs=(P(ROW, COL, None), P(), P(), P(), P(), P(), P(ROW, COL), P(ROW, COL)),
        out_specs=(P(), P(ROW, COL, None), P(), P(), P(ROW + COL, None), P(ROW + COL, None), P()),
        check_vma=False,
    )
```

```python
import functools

import jax
import jax.numpy as jnp
from jax import lax
from jax.experimental import pallas as pl
from jax.experimental.pallas import tpu as pltpu
from jax.sharding import Mesh
from jax.sharding import PartitionSpec as P

AXES = ("yl", "x", "z", "yh", "co")
ROW = ("yl", "x")
COL = ("z", "yh", "co")
PLANE = ("yl", "x", "yh")

EPSILON = 1e-05
ROWS, COLS, C, H, BINS = 32, 8, 128, 512, 64
PAIRS = ROWS * COLS
HALF = PAIRS // 2
F32, BF16 = jnp.float32, jnp.bfloat16
LAST = BINS - 1
MASK = BINS
BIG = 40
SMALL = 40
SLAB = 16 * BIG + SMALL


def split(value):
    high = value.astype(jnp.bfloat16)
    return high, (value - high.astype(jnp.float32)).astype(jnp.bfloat16)


def product(left, right, left_dim, right_dim):
    dims = (((left_dim,), (right_dim,)), ((), ()))
    return lax.dot_general(left, right, dims, preferred_element_type=F32)


def wide(left, right, left_dim, right_dim):
    both = product(left[0], jnp.concatenate(right, axis=1 - right_dim), left_dim, right_dim)
    return both[:, :C] + (both[:, C:] + product(left[1], right[0], left_dim, right_dim))


def deep(left, right, right_dim):
    stacked = product(jnp.concatenate(left, axis=1), jnp.concatenate([right[0]] * 2, axis=right_dim), 1, right_dim)
    return stacked + product(left[0], right[1], 1, right_dim)


def norm(x):
    centred = x - jnp.mean(x, axis=-1, keepdims=True)
    scale = lax.rsqrt(jnp.mean(centred * centred, axis=-1, keepdims=True) + EPSILON)
    return scale, centred * scale


def load_kernel(
    x_hbm, gain_hbm, bias_hbm, labels_hbm, mask_hbm, w_pde_hbm, w_in_hbm, w_out_hbm,
    x_ref, gain, bias, code, w_pde, in_high, in_low, out_high, out_low, w_in, w_out, labels, mask, sems,
):
    rows = pl.ds(pl.multiple_of(lax.axis_index("co") * HALF, HALF), HALF)
    ins = (w_in_hbm, w_out_hbm, x_hbm.at[rows, :], gain_hbm, bias_hbm, labels_hbm, mask_hbm, w_pde_hbm)
    refs = (w_in, w_out, x_ref, gain, bias, labels, mask, w_pde)
    copies = [pltpu.make_async_copy(i, r, sems.at[k]) for k, (i, r) in enumerate(zip(ins, refs))]
    for copy in copies:
        copy.start()
    copies[0].wait()
    in_high[...], in_low[...] = split(w_in[...])
    copies[1].wait()
    out_high[...], out_low[...] = split(w_out[...])
    for copy in copies[2:]:
        copy.wait()
    code[...] = (labels[...] + 64 * mask[...]).astype(F32)


def forward_kernel(
    x_other, x_ref, gain, bias, w_pde, in_high, in_low, out_high, out_low,
    scores_ref, updated_high, updated_low, unit_ref, scale_ref, normed_high, normed_low,
    silu_ref, slope_ref, hidden_high, hidden_low,
):
    core = lax.axis_index("co")
    first = core == 0
    rows = pl.ds(pl.multiple_of(core * HALF, HALF), HALF)
    mine, other = x_ref[...], x_other[rows, :]
    x = jnp.concatenate([jnp.where(first, mine, other), jnp.where(first, other, mine)], axis=0)
    scale, unit = norm(x)
    unit_ref[...] = unit
    scale_ref[...] = jnp.broadcast_to(scale, (PAIRS, C))
    normed = split(unit * gain[...] + bias[...])
    normed_high[...], normed_low[...] = normed
    projected_in = deep(normed, (in_high[...], in_low[...]), 1)
    gate, up = projected_in[:, :H], projected_in[:, H:]
    sigmoid = 1.0 / (1.0 + jnp.exp(-gate))
    silu = gate * sigmoid
    silu_ref[...] = silu
    slope_ref[...] = up * (sigmoid * (1.0 + gate * (1.0 - sigmoid)))
    hidden = split(silu * up)
    hidden_high[...], hidden_low[...] = hidden
    updated = split(x + wide(hidden, (out_high[...], out_low[...]), 1, 0))
    updated_high[...], updated_low[...] = updated
    high, low = split(w_pde[...])
    weights = jnp.concatenate(
        [jnp.concatenate([high, high], axis=1), jnp.concatenate([low, jnp.zeros_like(low)], axis=1)], axis=0
    )
    projected = product(jnp.concatenate(updated, axis=1), weights, 1, 1)
    projected = projected + pltpu.roll(projected, BINS, 1)
    scores_ref[...] = projected - projected[:, LAST:BINS]


def pack_kernel(scores_ref, code_ref, code_other, send, own):
    core = lax.axis_index("co")
    first = core == 0
    mine, other = code_ref[...], code_other[...]
    pair = lax.broadcasted_iota(jnp.int32, (HALF, ROWS), 0)
    row = lax.broadcasted_iota(jnp.int32, (HALF, ROWS), 1)
    spread = jnp.where(pair // COLS + 16 * core == row, 1.0, 0.0).astype(BF16)
    codes = (jnp.where(first, mine, other), jnp.where(first, other, mine))
    by_row = jnp.concatenate([product(spread, code.astype(BF16), 1, 1) for code in codes], axis=0)
    pair = lax.broadcasted_iota(jnp.int32, (PAIRS, COLS), 0)
    col = lax.broadcasted_iota(jnp.int32, (PAIRS, COLS), 1)
    code = jnp.sum(jnp.where(pair % COLS == col, by_row, 0.0), axis=1, keepdims=True)
    scored = jnp.where(code >= 64.0, 1.0, 0.0)
    lane = lax.broadcasted_iota(jnp.int32, (PAIRS, C), 1)
    projected = jnp.where(lane < LAST, scores_ref[...], jnp.where(lane == LAST, code - 64.0 * scored, scored))
    own[...] = projected
    send[...] = jnp.where(lane[:HALF] < BINS, projected[:HALF], pltpu.roll(projected[HALF:], BINS, 1))


def backward_kernel(
    received, gain, w_pde, in_high, in_low, out_high, out_low, own, updated_high, updated_low, unit_ref, scale_ref,
    normed_high, normed_low, silu_ref, slope_ref, hidden_high, hidden_low,
    send, keep, d_x_ref, flat_ref, mirrored_ref,
):
    core = lax.axis_index("co")
    first = core == 0
    flat_ref[0:HALF, :] = received[...]
    flat_ref[HALF:PAIRS, :] = pltpu.roll(received[...], BINS, 1)
    for half in range(2):
        for row in range(16):
            start = HALF * (row // 8) + 64 * half + row % 8
            mirrored_ref[HALF * half + 8 * row : HALF * half + 8 * row + 8, :] = flat_ref[pl.ds(start, 8, stride=8), :]
    mine, mirrored = own[...], mirrored_ref[...]
    lane = lax.broadcasted_iota(jnp.int32, (PAIRS, C), 1)
    lane_float = lane.astype(jnp.float32)
    scored = mine[:, MASK : MASK + 1]
    onehot = lane_float == mine[:, LAST:BINS]
    onehot_mirrored = lane_float == mirrored[:, LAST:BINS]
    scores = jnp.where(lane < LAST, mine + mirrored, jnp.where(lane == LAST, 0.0, -jnp.inf))
    highest = jnp.max(scores, axis=1, keepdims=True)
    shifted = jnp.exp(scores - highest)
    total = jnp.sum(shifted, axis=1, keepdims=True)
    picked = jnp.sum(jnp.where(onehot, scores, 0.0), axis=1, keepdims=True)
    loss = jnp.sum(scored * (highest + jnp.log(total) - picked))
    count = jnp.sum(scored)
    labelled = jnp.where(onehot, 1.0, 0.0) + jnp.where(onehot_mirrored, 1.0, 0.0)
    d_sym = scored * (shifted * (2.0 / total) - labelled)
    high = d_sym.astype(BF16)
    rest = d_sym - high.astype(F32)
    packed = jnp.where(lane < BINS, high.astype(F32), pltpu.roll(rest, BINS, 1)).astype(BF16)

    high_pde, low_pde = split(w_pde[...])
    weights = jnp.concatenate([high_pde, high_pde, low_pde, jnp.zeros_like(low_pde)], axis=0)
    d_updated = product(jnp.concatenate([packed, high], axis=1), weights, 1, 0)
    d_pde = product(packed, jnp.concatenate([updated_high[...], updated_low[...]], axis=1), 0, 0)
    d_pde = d_pde[:BINS, :C] + (d_pde[:BINS, C:] + d_pde[BINS:, :C])
    d_out = product(hidden_high[...], packed, 0, 0)
    d_out = d_out + (pltpu.roll(d_out, BINS, 1) + product(hidden_low[...], high, 0, 0))
    d_hidden = deep(split(d_updated), (out_high[...], out_low[...]), 1)
    d_in_gate = split(d_hidden * slope_ref[...])
    d_in_up = split(d_hidden * silu_ref[...])
    normed = normed_high[...], normed_low[...]
    d_gate = wide(d_in_gate, normed, 0, 0)
    d_up = wide(d_in_up, normed, 0, 0)
    d_normed = wide(d_in_gate, (in_high[:H], in_low[:H]), 1, 0) + wide(d_in_up, (in_high[H:], in_low[H:]), 1, 0)
    unit = unit_ref[...]
    d_unit = d_normed * gain[...]
    d_x = d_updated + scale_ref[...] * (
        d_unit - jnp.mean(d_unit, axis=1, keepdims=True) - unit * jnp.mean(d_unit * unit, axis=1, keepdims=True)
    )

    sub = lax.broadcasted_iota(jnp.int32, (8, C), 0)
    lane = lax.broadcasted_iota(jnp.int32, (8, C), 1)
    d_x_ref[...] = jnp.where(first, d_x[:HALF], d_x[HALF:])
    send[SLAB : SLAB + HALF, :] = jnp.where(first, d_x[HALF:], d_x[:HALF])

    def put(rows, lows, highs):
        keep[rows : rows + 8, :] = jnp.where(first, lows, highs)
        send[rows : rows + 8, :] = jnp.where(first, highs, lows)

    d_out_tiles = [
        [
            jnp.where(
                lane < BINS,
                d_out[(8 * k + low) * 8 : (8 * k + low) * 8 + 8],
                pltpu.roll(d_out[(8 * k + 4 + low) * 8 : (8 * k + 4 + low) * 8 + 8], BINS, 1),
            )
            for low in range(4)
        ]
        for k in range(8)
    ]
    for yl, d_half in ((0, d_gate), (1, d_up)):
        for xx in range(4):
            for yh in range(2):
                start = ((yl * 4 + xx) * 2 + yh) * BIG
                for m in range(4):
                    one = (xx * 8 + 2 * m) * 16 + yh * 8
                    even, odd = d_half[one : one + 8], d_half[one + 16 : one + 24]
                    lows = jnp.where(sub < 4, even, pltpu.roll(odd, 4, 0))
                    highs = jnp.where(sub < 4, pltpu.roll(even, 4, 0), odd)
                    put(start + 8 * m, lows, highs)
                cores = []
                for cc in range(2):
                    tile = None
                    for low, piece in enumerate(d_out_tiles[yl * 4 + xx]):
                        shift = (2 * low - 4 * yh - 2 * cc) % 8
                        piece = pltpu.roll(piece, shift, 0) if shift else piece
                        tile = piece if low == 0 else jnp.where(sub < 2 * low, tile, piece)
                    cores.append(tile)
                put(start + 32, *cores)
    for k in range(4):
        put(16 * BIG + 8 * k, d_pde[8 * k : 8 * k + 8], d_pde[32 + 8 * k : 40 + 8 * k])
    d_gain = jnp.sum(d_normed * unit, axis=0, keepdims=True)
    d_bias = jnp.sum(d_normed, axis=0, keepdims=True)
    tail = jnp.where(sub == 0, d_gain, jnp.where(sub == 1, d_bias, 0.0))
    tail = jnp.where((sub == 2) & (lane == 0), loss, tail)
    tail = jnp.where((sub == 2) & (lane == 1), count, tail)
    put(16 * BIG + 32, tail, tail)


def core_sum_kernel(keep, received, send):
    total = keep[...] + received[0:SLAB]
    for d in range(16):
        send[d, 0:BIG, :] = total[d * BIG : (d + 1) * BIG]
        send[d, BIG : BIG + SMALL, :] = total[16 * BIG :]


def plane_sum_kernel(received, send):
    total = received[0]
    for d in range(1, 16):
        total = total + received[d]
    tail = total[BIG + 32 : BIG + 35]
    lane = lax.broadcasted_iota(jnp.int32, (2, C), 1)
    measures = pltpu.roll(jnp.broadcast_to(tail[2:3], (8, C)), BINS, 1)[0:2]
    for z in range(8):
        send[z, 0:4, :] = total[4 * z : 4 * z + 4]
        pair = total[32 + 2 * (z % 4) : 34 + 2 * (z % 4)]
        pair = pltpu.roll(jnp.concatenate([pair] * 4, axis=0), BINS, 1)[0:2] if z >= 4 else pair
        send[z, 4:6, :] = jnp.where(lane < BINS, pair, measures)
        send[z, 6:8, :] = tail[0:2]
        send[z, 8:40, :] = total[BIG : BIG + 32]


def pde_sum_kernel(received, d_pde):
    total = received[0]
    for d in range(1, 8):
        total = total + received[d]
    d_pde[...] = total[8:40] * (1.0 / total[4:5, BINS + 1 : BINS + 2])


def column_sum_kernel(received, w_pde, d_x, d_x_other, loss, d_gain, d_bias, d_in, d_out, d_x_out):
    total = received[0, 0:8]
    for d in range(1, 8):
        total = total + received[d, 0:8]
    count = total[4:5, BINS + 1 : BINS + 2]
    inverse = 1.0 / count
    loss[...] = total[4:5, BINS : BINS + 1] / count
    d_in[...] = total[0:4] * inverse
    d_gain[...] = total[6:7] * inverse
    d_bias[...] = total[7:8] * inverse
    left, right = split(total[:, :BINS]), split(w_pde[...])
    projected = product(left[0], right[0], 1, 0) + (product(left[0], right[1], 1, 0) + product(left[1], right[0], 1, 0))
    d_out[...] = projected[4:6] * inverse
    first = lax.axis_index("co") == 0
    mine, other = d_x[...] * inverse, d_x_other[SLAB : SLAB + HALF] * inverse
    d_x_out[0:HALF, :] = jnp.where(first, mine, other)
    d_x_out[HALF:PAIRS, :] = jnp.where(first, other, mine)


def join_kernel(mine, other, out):
    first = lax.axis_index("co") == 0
    out[0:32, :] = jnp.where(first, mine[...], other[...])
    out[32:64, :] = jnp.where(first, other[...], mine[...])


VMEM = pl.BlockSpec(memory_space=pltpu.VMEM)
HBM = pl.BlockSpec(memory_space=pltpu.HBM)


def call(kernel, outs, in_specs, scratch=(), name=None, limit=12):
    outs = [out if isinstance(out[0], tuple) else (out, F32) for out in outs]
    shapes = [jax.ShapeDtypeStruct(*out) for out in outs]
    return pl.pallas_call(
        kernel,
        out_shape=shapes,
        in_specs=in_specs,
        out_specs=[VMEM] * len(outs),
        scratch_shapes=list(scratch),
        compiler_params=pltpu.CompilerParams(vmem_limit_bytes=limit << 20),
        name=name,
    )


def mirror_pairs():
    return [
        (r * 32 + z * 4 + yh * 2 + co, z * 32 + r * 4 + co * 2 + yh)
        for r in range(8)
        for z in range(8)
        for yh in range(2)
        for co in range(2)
    ]


def on_device(pair_rep, ln_gain, ln_bias, w_in, w_out, w_pde, labels, pair_mask):
    swap = [(0, 1), (1, 0)]
    x = pair_rep.reshape(PAIRS, C)
    gain, bias, w_pde, labels, mask = ln_gain.reshape(1, C), ln_bias.reshape(1, C), w_pde.T, labels.T, pair_mask.T
    x_other = lax.ppermute(x, "co", swap)
    full, half = (PAIRS, C), (PAIRS, H)
    in_hbm = functools.partial(pltpu.with_memory_space_constraint, memory_space=pltpu.HBM)
    x, gain, bias, code, *weights = call(
        load_kernel,
        [(HALF, C), (1, C), (1, C), (COLS, ROWS), (BINS, C)]
        + [((2 * H, C), BF16)] * 2
        + [((H, C), BF16)] * 2,
        [HBM] * 8,
        scratch=[pltpu.VMEM((2 * H, C), F32), pltpu.VMEM((H, C), F32)]
        + [pltpu.VMEM((COLS, ROWS), jnp.int32)] * 2
        + [pltpu.SemaphoreType.DMA((8,))],
        name="load",
    )(*(in_hbm(a) for a in (x, gain, bias, labels, mask, w_pde, w_in, w_out)))
    code_other = lax.ppermute(code, "co", swap)
    scores, *kept = call(
        forward_kernel,
        [full, (full, BF16), (full, BF16), full, full, (full, BF16), (full, BF16)] + [half, half, (half, BF16), (half, BF16)],
        [VMEM] * 9,
        name="forward",
    )(x_other, x, gain, bias, *weights)
    send, own = call(pack_kernel, [(HALF, C), full], [VMEM] * 3, name="pack")(scores, code, code_other)
    received = lax.ppermute(send, AXES, mirror_pairs())
    send, keep, d_x = call(
        backward_kernel,
        [(SLAB + HALF, C), (SLAB, C), (HALF, C)],
        [VMEM] * 18,
        scratch=[pltpu.VMEM(full, F32)] * 2,
        name="backward",
    )(received, gain, *weights, own, *kept)
    from_core = lax.ppermute(send, "co", swap)
    (send,) = call(core_sum_kernel, [(16, BIG + SMALL, C)], [VMEM] * 2, name="core_sum")(keep, from_core)
    received = lax.all_to_all(send, PLANE, 0, 0, tiled=True)
    (send,) = call(plane_sum_kernel, [(8, 40, C)], [VMEM], name="plane_sum")(received)
    received = lax.all_to_all(send, "z", 0, 0, tiled=True)
    (d_pde,) = call(pde_sum_kernel, [(32, C)], [VMEM], name="pde_sum")(received)
    other = lax.ppermute(d_pde, "co", swap)
    loss, d_gain, d_bias, d_in, d_out, d_x = call(
        column_sum_kernel,
        [(1, 1), (1, C), (1, C), (4, C), (2, C), full],
        [VMEM] * 4,
        name="column_sum",
    )(received, weights[0], d_x, from_core)
    (d_pde,) = call(join_kernel, [(BINS, C)], [VMEM] * 2, name="join")(d_pde, other)
    return (
        loss.reshape(()),
        d_x.reshape(ROWS, COLS, C),
        d_gain.reshape(C),
        d_bias.reshape(C),
        d_in,
        d_out,
        d_pde.T,
    )


def solution(mesh):
    torus = Mesh(mesh.devices.reshape(2, 4, 8, 2, 2), AXES)
    return jax.shard_map(
        on_device,
        mesh=torus,
        in_specs=(P(ROW, COL, None), P(), P(), P(), P(), P(), P(ROW, COL), P(ROW, COL)),
        out_specs=(P(), P(ROW, COL, None), P(), P(), P(ROW + COL, None), P(ROW + COL, None), P()),
        check_vma=False,
    )
```

```python
import functools

import jax
import jax.numpy as jnp
from jax import lax
from jax.experimental import pallas as pl
from jax.experimental.pallas import tpu as pltpu
from jax.sharding import Mesh
from jax.sharding import PartitionSpec as P

AXES = ("yl", "x", "z", "yh", "co")
ROW = ("yl", "x")
COL = ("z", "yh", "co")
PLANE = ("yl", "x", "yh")

EPSILON = 1e-05
ROWS, COLS, C, H, BINS = 32, 8, 128, 512, 64
PAIRS = ROWS * COLS
HALF = PAIRS // 2
F32, BF16 = jnp.float32, jnp.bfloat16
LAST = BINS - 1
BIG = 40
SMALL = 40
SLAB = 16 * BIG + SMALL


def split(value):
    high = value.astype(jnp.bfloat16)
    return high, (value - high.astype(jnp.float32)).astype(jnp.bfloat16)


def product(left, right, left_dim, right_dim):
    dims = (((left_dim,), (right_dim,)), ((), ()))
    return lax.dot_general(left, right, dims, preferred_element_type=F32)


def wide(left, right, left_dim, right_dim):
    both = product(left[0], jnp.concatenate(right, axis=1 - right_dim), left_dim, right_dim)
    return both[:, :C] + (both[:, C:] + product(left[1], right[0], left_dim, right_dim))


def deep(left, right, right_dim):
    stacked = product(jnp.concatenate(left, axis=1), jnp.concatenate([right[0]] * 2, axis=right_dim), 1, right_dim)
    return stacked + product(left[0], right[1], 1, right_dim)


def norm(x):
    centred = x - jnp.mean(x, axis=-1, keepdims=True)
    scale = lax.rsqrt(jnp.mean(centred * centred, axis=-1, keepdims=True) + EPSILON)
    return scale, centred * scale


def load_kernel(
    x_hbm, gain_hbm, bias_hbm, labels_hbm, mask_hbm, w_pde_hbm, w_in_hbm, w_out_hbm,
    x_ref, gain, bias, labels, mask, w_pde, in_high, in_low, out_high, out_low, w_in, w_out, sems,
):
    rows = pl.ds(pl.multiple_of(lax.axis_index("co") * HALF, HALF), HALF)
    ins = (w_in_hbm, w_out_hbm, x_hbm.at[rows, :], gain_hbm, bias_hbm, labels_hbm, mask_hbm, w_pde_hbm)
    refs = (w_in, w_out, x_ref, gain, bias, labels, mask, w_pde)
    copies = [pltpu.make_async_copy(i, r, sems.at[k]) for k, (i, r) in enumerate(zip(ins, refs))]
    for copy in copies:
        copy.start()
    copies[0].wait()
    in_high[...], in_low[...] = split(w_in[...])
    copies[1].wait()
    out_high[...], out_low[...] = split(w_out[...])
    for copy in copies[2:]:
        copy.wait()


def spread_pairs(mine, other):
    core = lax.axis_index("co")
    first = core == 0
    pair = lax.broadcasted_iota(jnp.int32, (HALF, ROWS), 0)
    row = lax.broadcasted_iota(jnp.int32, (HALF, ROWS), 1)
    spread = jnp.where(pair // COLS + 16 * core == row, 1.0, 0.0).astype(BF16)
    mine, other = mine.astype(F32), other.astype(F32)
    parts = (jnp.where(first, mine, other), jnp.where(first, other, mine))
    by_row = jnp.concatenate([product(spread, part.astype(BF16), 1, 1) for part in parts], axis=0)
    pair = lax.broadcasted_iota(jnp.int32, (PAIRS, COLS), 0)
    col = lax.broadcasted_iota(jnp.int32, (PAIRS, COLS), 1)
    return jnp.sum(jnp.where(pair % COLS == col, by_row, 0.0), axis=1, keepdims=True)


def scored_kernel(mask, mask_other, scored):
    scored[...] = jnp.broadcast_to(spread_pairs(mask[...], mask_other[...]), (PAIRS, C))


def forward_kernel(
    x_other, labels_other, x_ref, gain, bias, labels, mask, w_pde, in_high, in_low, out_high, out_low,
    send, mask_out, own, updated_high, updated_low, unit_ref, scale_ref, normed_high, normed_low,
    silu_ref, slope_ref, hidden_high, hidden_low,
):
    core = lax.axis_index("co")
    first = core == 0
    rows = pl.ds(pl.multiple_of(core * HALF, HALF), HALF)
    mine, other = x_ref[...], x_other[rows, :]
    x = jnp.concatenate([jnp.where(first, mine, other), jnp.where(first, other, mine)], axis=0)
    scale, unit = norm(x)
    unit_ref[...] = unit
    scale_ref[...] = jnp.broadcast_to(scale, (PAIRS, C))
    normed = split(unit * gain[...] + bias[...])
    normed_high[...], normed_low[...] = normed
    mask_out[...] = mask[...]
    label = spread_pairs(labels[...], labels_other[...])
    projected_in = deep(normed, (in_high[...], in_low[...]), 1)
    gate, up = projected_in[:, :H], projected_in[:, H:]
    sigmoid = 1.0 / (1.0 + jnp.exp(-gate))
    silu = gate * sigmoid
    silu_ref[...] = silu
    slope_ref[...] = up * (sigmoid * (1.0 + gate * (1.0 - sigmoid)))
    hidden = split(silu * up)
    hidden_high[...], hidden_low[...] = hidden
    updated = split(x + wide(hidden, (out_high[...], out_low[...]), 1, 0))
    updated_high[...], updated_low[...] = updated
    high, low = split(w_pde[...])
    weights = jnp.concatenate(
        [jnp.concatenate([high, high], axis=1), jnp.concatenate([low, jnp.zeros_like(low)], axis=1)], axis=0
    )
    projected = product(jnp.concatenate(updated, axis=1), weights, 1, 1)
    projected = projected + pltpu.roll(projected, BINS, 1)
    lane = lax.broadcasted_iota(jnp.int32, (PAIRS, C), 1)
    projected = projected - projected[:, LAST:BINS]
    projected = jnp.where(lane < LAST, projected, label)
    own[...] = projected
    send[...] = jnp.where(lane[:HALF] < BINS, projected[:HALF], pltpu.roll(projected[HALF:], BINS, 1))


def backward_kernel(
    received, scored_ref, gain, w_pde, in_high, in_low, out_high, out_low, own, updated_high, updated_low, unit_ref, scale_ref,
    normed_high, normed_low, silu_ref, slope_ref, hidden_high, hidden_low,
    send, keep, d_x_ref, flat_ref, mirrored_ref,
):
    core = lax.axis_index("co")
    first = core == 0
    flat_ref[0:HALF, :] = received[...]
    flat_ref[HALF:PAIRS, :] = pltpu.roll(received[...], BINS, 1)
    for half in range(2):
        for row in range(16):
            start = HALF * (row // 8) + 64 * half + row % 8
            mirrored_ref[HALF * half + 8 * row : HALF * half + 8 * row + 8, :] = flat_ref[pl.ds(start, 8, stride=8), :]
    mine, mirrored = own[...], mirrored_ref[...]
    lane = lax.broadcasted_iota(jnp.int32, (PAIRS, C), 1)
    lane_float = lane.astype(jnp.float32)
    scored = scored_ref[:, 0:1]
    onehot = lane_float == mine[:, LAST:BINS]
    onehot_mirrored = lane_float == mirrored[:, LAST:BINS]
    scores = jnp.where(lane < LAST, mine + mirrored, jnp.where(lane == LAST, 0.0, -jnp.inf))
    highest = jnp.max(scores, axis=1, keepdims=True)
    shifted = jnp.exp(scores - highest)
    total = jnp.sum(shifted, axis=1, keepdims=True)
    picked = jnp.sum(jnp.where(onehot, scores, 0.0), axis=1, keepdims=True)
    loss = jnp.sum(scored * (highest + jnp.log(total) - picked))
    count = jnp.sum(scored)
    labelled = jnp.where(onehot, 1.0, 0.0) + jnp.where(onehot_mirrored, 1.0, 0.0)
    d_sym = scored * (shifted * (2.0 / total) - labelled)
    high = d_sym.astype(BF16)
    rest = d_sym - high.astype(F32)
    packed = jnp.where(lane < BINS, high.astype(F32), pltpu.roll(rest, BINS, 1)).astype(BF16)

    high_pde, low_pde = split(w_pde[...])
    weights = jnp.concatenate([high_pde, high_pde, low_pde, jnp.zeros_like(low_pde)], axis=0)
    d_updated = product(jnp.concatenate([packed, high], axis=1), weights, 1, 0)
    d_pde = product(packed, jnp.concatenate([updated_high[...], updated_low[...]], axis=1), 0, 0)
    d_pde = d_pde[:BINS, :C] + (d_pde[:BINS, C:] + d_pde[BINS:, :C])
    d_out = product(hidden_high[...], packed, 0, 0)
    d_out = d_out + (pltpu.roll(d_out, BINS, 1) + product(hidden_low[...], high, 0, 0))
    d_hidden = deep(split(d_updated), (out_high[...], out_low[...]), 1)
    d_in_gate = split(d_hidden * slope_ref[...])
    d_in_up = split(d_hidden * silu_ref[...])
    normed = normed_high[...], normed_low[...]
    d_gate = wide(d_in_gate, normed, 0, 0)
    d_up = wide(d_in_up, normed, 0, 0)
    d_normed = wide(d_in_gate, (in_high[:H], in_low[:H]), 1, 0) + wide(d_in_up, (in_high[H:], in_low[H:]), 1, 0)
    unit = unit_ref[...]
    d_unit = d_normed * gain[...]
    d_x = d_updated + scale_ref[...] * (
        d_unit - jnp.mean(d_unit, axis=1, keepdims=True) - unit * jnp.mean(d_unit * unit, axis=1, keepdims=True)
    )

    sub = lax.broadcasted_iota(jnp.int32, (8, C), 0)
    lane = lax.broadcasted_iota(jnp.int32, (8, C), 1)
    d_x_ref[...] = jnp.where(first, d_x[:HALF], d_x[HALF:])
    send[SLAB : SLAB + HALF, :] = jnp.where(first, d_x[HALF:], d_x[:HALF])

    def put(rows, lows, highs):
        keep[rows : rows + 8, :] = jnp.where(first, lows, highs)
        send[rows : rows + 8, :] = jnp.where(first, highs, lows)

    d_out_tiles = [
        [
            jnp.where(
                lane < BINS,
                d_out[(8 * k + low) * 8 : (8 * k + low) * 8 + 8],
                pltpu.roll(d_out[(8 * k + 4 + low) * 8 : (8 * k + 4 + low) * 8 + 8], BINS, 1),
            )
            for low in range(4)
        ]
        for k in range(8)
    ]
    for yl, d_half in ((0, d_gate), (1, d_up)):
        for xx in range(4):
            for yh in range(2):
                start = ((yl * 4 + xx) * 2 + yh) * BIG
                for m in range(4):
                    one = (xx * 8 + 2 * m) * 16 + yh * 8
                    even, odd = d_half[one : one + 8], d_half[one + 16 : one + 24]
                    lows = jnp.where(sub < 4, even, pltpu.roll(odd, 4, 0))
                    highs = jnp.where(sub < 4, pltpu.roll(even, 4, 0), odd)
                    put(start + 8 * m, lows, highs)
                cores = []
                for cc in range(2):
                    tile = None
                    for low, piece in enumerate(d_out_tiles[yl * 4 + xx]):
                        shift = (2 * low - 4 * yh - 2 * cc) % 8
                        piece = pltpu.roll(piece, shift, 0) if shift else piece
                        tile = piece if low == 0 else jnp.where(sub < 2 * low, tile, piece)
                    cores.append(tile)
                put(start + 32, *cores)
    for k in range(4):
        put(16 * BIG + 8 * k, d_pde[8 * k : 8 * k + 8], d_pde[32 + 8 * k : 40 + 8 * k])
    d_gain = jnp.sum(d_normed * unit, axis=0, keepdims=True)
    d_bias = jnp.sum(d_normed, axis=0, keepdims=True)
    tail = jnp.where(sub == 0, d_gain, jnp.where(sub == 1, d_bias, 0.0))
    tail = jnp.where((sub == 2) & (lane == 0), loss, tail)
    tail = jnp.where((sub == 2) & (lane == 1), count, tail)
    put(16 * BIG + 32, tail, tail)


def core_sum_kernel(keep, received, send):
    total = keep[...] + received[0:SLAB]
    for d in range(16):
        send[d, 0:BIG, :] = total[d * BIG : (d + 1) * BIG]
        send[d, BIG : BIG + SMALL, :] = total[16 * BIG :]


def plane_sum_kernel(received, send):
    total = received[0]
    for d in range(1, 16):
        total = total + received[d]
    tail = total[BIG + 32 : BIG + 35]
    lane = lax.broadcasted_iota(jnp.int32, (2, C), 1)
    measures = pltpu.roll(jnp.broadcast_to(tail[2:3], (8, C)), BINS, 1)[0:2]
    for z in range(8):
        send[z, 0:4, :] = total[4 * z : 4 * z + 4]
        pair = total[32 + 2 * (z % 4) : 34 + 2 * (z % 4)]
        pair = pltpu.roll(jnp.concatenate([pair] * 4, axis=0), BINS, 1)[0:2] if z >= 4 else pair
        send[z, 4:6, :] = jnp.where(lane < BINS, pair, measures)
        send[z, 6:8, :] = tail[0:2]
        send[z, 8:40, :] = total[BIG : BIG + 32]


def pde_sum_kernel(received, d_pde):
    total = received[0]
    for d in range(1, 8):
        total = total + received[d]
    d_pde[...] = total[8:40] * (1.0 / total[4:5, BINS + 1 : BINS + 2])


def column_sum_kernel(received, w_pde, d_x, d_x_other, loss, d_gain, d_bias, d_in, d_out, d_x_out):
    total = received[0, 0:8]
    for d in range(1, 8):
        total = total + received[d, 0:8]
    count = total[4:5, BINS + 1 : BINS + 2]
    inverse = 1.0 / count
    loss[...] = total[4:5, BINS : BINS + 1] / count
    d_in[...] = total[0:4] * inverse
    d_gain[...] = total[6:7] * inverse
    d_bias[...] = total[7:8] * inverse
    left, right = split(total[:, :BINS]), split(w_pde[...])
    projected = product(left[0], right[0], 1, 0) + (product(left[0], right[1], 1, 0) + product(left[1], right[0], 1, 0))
    d_out[...] = projected[4:6] * inverse
    first = lax.axis_index("co") == 0
    mine, other = d_x[...] * inverse, d_x_other[SLAB : SLAB + HALF] * inverse
    d_x_out[0:HALF, :] = jnp.where(first, mine, other)
    d_x_out[HALF:PAIRS, :] = jnp.where(first, other, mine)


def join_kernel(mine, other, out):
    first = lax.axis_index("co") == 0
    out[0:32, :] = jnp.where(first, mine[...], other[...])
    out[32:64, :] = jnp.where(first, other[...], mine[...])


VMEM = pl.BlockSpec(memory_space=pltpu.VMEM)
HBM = pl.BlockSpec(memory_space=pltpu.HBM)


def call(kernel, outs, in_specs, scratch=(), name=None, limit=12):
    outs = [out if isinstance(out[0], tuple) else (out, F32) for out in outs]
    shapes = [jax.ShapeDtypeStruct(*out) for out in outs]
    return pl.pallas_call(
        kernel,
        out_shape=shapes,
        in_specs=in_specs,
        out_specs=[VMEM] * len(outs),
        scratch_shapes=list(scratch),
        compiler_params=pltpu.CompilerParams(vmem_limit_bytes=limit << 20),
        name=name,
    )


def mirror_pairs():
    return [
        (r * 32 + z * 4 + yh * 2 + co, z * 32 + r * 4 + co * 2 + yh)
        for r in range(8)
        for z in range(8)
        for yh in range(2)
        for co in range(2)
    ]


def on_device(pair_rep, ln_gain, ln_bias, w_in, w_out, w_pde, labels, pair_mask):
    swap = [(0, 1), (1, 0)]
    x = pair_rep.reshape(PAIRS, C)
    gain, bias, w_pde, labels, mask = ln_gain.reshape(1, C), ln_bias.reshape(1, C), w_pde.T, labels.T, pair_mask.T
    x_other, labels_other = (lax.ppermute(a, "co", swap) for a in (x, labels))
    full, half = (PAIRS, C), (PAIRS, H)
    in_hbm = functools.partial(pltpu.with_memory_space_constraint, memory_space=pltpu.HBM)
    x, gain, bias, labels, mask, *weights = call(
        load_kernel,
        [(HALF, C), (1, C), (1, C), ((COLS, ROWS), jnp.int32), ((COLS, ROWS), jnp.int32), (BINS, C)]
        + [((2 * H, C), BF16)] * 2
        + [((H, C), BF16)] * 2,
        [HBM] * 8,
        scratch=[pltpu.VMEM((2 * H, C), F32), pltpu.VMEM((H, C), F32), pltpu.SemaphoreType.DMA((8,))],
        name="load",
    )(*(in_hbm(a) for a in (x, gain, bias, labels, mask, w_pde, w_in, w_out)))
    send, mask, *kept = call(
        forward_kernel,
        [(HALF, C), ((COLS, ROWS), jnp.int32), full, (full, BF16), (full, BF16), full, full, (full, BF16), (full, BF16)]
        + [half, half, (half, BF16), (half, BF16)],
        [VMEM] * 12,
        name="forward",
    )(x_other, labels_other, x, gain, bias, labels, mask, *weights)
    received = lax.ppermute(send, AXES, mirror_pairs())
    mask_other = lax.ppermute(mask, "co", swap)
    (scored,) = call(scored_kernel, [full], [VMEM] * 2, name="scored")(mask, mask_other)
    send, keep, d_x = call(
        backward_kernel,
        [(SLAB + HALF, C), (SLAB, C), (HALF, C)],
        [VMEM] * 19,
        scratch=[pltpu.VMEM(full, F32)] * 2,
        name="backward",
    )(received, scored, gain, *weights, *kept)
    from_core = lax.ppermute(send, "co", swap)
    (send,) = call(core_sum_kernel, [(16, BIG + SMALL, C)], [VMEM] * 2, name="core_sum")(keep, from_core)
    received = lax.all_to_all(send, PLANE, 0, 0, tiled=True)
    (send,) = call(plane_sum_kernel, [(8, 40, C)], [VMEM], name="plane_sum")(received)
    received = lax.all_to_all(send, "z", 0, 0, tiled=True)
    (d_pde,) = call(pde_sum_kernel, [(32, C)], [VMEM], name="pde_sum")(received)
    other = lax.ppermute(d_pde, "co", swap)
    loss, d_gain, d_bias, d_in, d_out, d_x = call(
        column_sum_kernel,
        [(1, 1), (1, C), (1, C), (4, C), (2, C), full],
        [VMEM] * 4,
        name="column_sum",
    )(received, weights[0], d_x, from_core)
    (d_pde,) = call(join_kernel, [(BINS, C)], [VMEM] * 2, name="join")(d_pde, other)
    return (
        loss.reshape(()),
        d_x.reshape(ROWS, COLS, C),
        d_gain.reshape(C),
        d_bias.reshape(C),
        d_in,
        d_out,
        d_pde.T,
    )


def solution(mesh):
    torus = Mesh(mesh.devices.reshape(2, 4, 8, 2, 2), AXES)
    return jax.shard_map(
        on_device,
        mesh=torus,
        in_specs=(P(ROW, COL, None), P(), P(), P(), P(), P(), P(ROW, COL), P(ROW, COL)),
        out_specs=(P(), P(ROW, COL, None), P(), P(), P(ROW + COL, None), P(ROW + COL, None), P()),
        check_vma=False,
    )
```
